512 devices in a mesh: doc: 64 (over y, z), qry: 8 (over x, core).
Axes of the slice: x: 4, y: 4, z: 16, core: 2. Of those that a mesh axis runs over, the one named last changes fastest.
Arguments:
- queries: bfloat16 [256, 4096], P('qry'), may hold values from -14 to 14
- passages: bfloat16 [69632, 4096], P(('doc', 'qry')), may hold values from -14 to 14
- passage_route: int32 [69632], P(('doc', 'qry')), may hold values from 0 to 131071, as said below
- pattern: int32 [8, 512], replicated, may hold values from 0 to 1, as said below
- teacher: float32 [256, 8192], P(None, ('doc', 'qry')), may hold values from -20 to 270
Outputs:
- doc_scores: float32 [256, 8192], P(None, ('doc', 'qry'))
- divergence: float32 [256], P('qry')
The draws below stay inside these ranges and needn't reach their ends.
Inputs may be any that keep to these rules, and one draw needn't show every extreme that they name: `passage_route`: A value v names document v // 16 (device g owns documents g * 16 to g * 16 + 15, with g = doc index * 8 + qry index) and passage v % 16 of it. Every document has 1 to 16 passages numbered from 0 without gaps, each held once over all shards, and its owner has the qry index of the shards that hold them. The passages of one owner are spread over the 64 shards of that qry index as evenly as possible (counts differ by at most one), so at most 4 go from one shard to one owner; in every qry index one owner holds 256 passages. Document t of the owner at doc index i and document t of the owner at doc index 63 - i, same qry index, have 16 + 1 passages together. `pattern`: entry [b, g] is 1 where queries b * 32 to b * 32 + 31 are scored against the documents of device g; every row has a 1.
All inputs are finite; a program needn't handle non-finite values.
Results may differ from the reference program's by a relative error of at most 0.0003.
Values may be sent and summed in bfloat16 or wider, within the bound.
A program may use at most 64 MiB of HBM per device.

```python
import math
import jax
import jax.numpy as jnp
from jax import lax

D = 4096
MAXP = 16
QRY_DEV = 32
DOC_DEV = 16
PP = 136
NQ = 256
NDOC = 8192
NP = 69632
N_DOC = 64
N_QRY = 8
DEVICES = 512


def route_table(key):
    base_key = jax.random.fold_in(key, 7001)
    keys = jax.random.split(base_key, 4)
    half_owners = N_DOC // 2
    shifts = jax.random.randint(keys[0], (N_QRY, half_owners, 1), -8, 9)
    hottest = jax.random.randint(keys[1], (N_QRY,), 0, half_owners)
    counts_low = jnp.clip(jax.random.randint(keys[2], (N_QRY, half_owners, DOC_DEV), 1, MAXP + 1) + shifts, 1, MAXP)
    owner_rank = jnp.arange(half_owners, dtype=jnp.int32)[None, :, None]
    counts_low = jnp.where(owner_rank == hottest[:, None, None], MAXP, counts_low)
    counts = jnp.concatenate([counts_low, (MAXP + 1 - counts_low)[:, ::-1, :]], axis=1)
    places = jnp.arange(MAXP, dtype=jnp.int32)[None, None, None, :]
    live = (places < counts[:, :, :, None]).astype(jnp.int32).reshape(N_QRY, -1)
    before = jnp.cumsum(live, axis=1) - live
    encoder_at = before % N_DOC
    local_at = before // N_DOC
    doc_index = jnp.arange(N_DOC, dtype=jnp.int32)[None, :, None, None]
    column_index = jnp.arange(N_QRY, dtype=jnp.int32)[:, None, None, None]
    within = jnp.arange(DOC_DEV, dtype=jnp.int32)[None, None, :, None]
    values = ((doc_index * N_QRY + column_index) * DOC_DEV + within) * MAXP + places
    values = jnp.broadcast_to(values, (N_QRY, N_DOC, DOC_DEV, MAXP)).reshape(N_QRY, -1)
    landing = jnp.where(live > 0, encoder_at * PP + local_at, N_DOC * PP)
    rows_of = jnp.arange(N_QRY, dtype=jnp.int32)[:, None]
    filled = jnp.zeros((N_QRY, N_DOC * PP + 1), jnp.int32).at[rows_of, landing].set(values)[:, :N_DOC * PP]
    filled = filled.reshape(N_QRY * N_DOC, PP)
    order_keys = jax.random.split(keys[3], N_QRY * N_DOC)
    orders = jax.vmap(lambda single: jax.random.permutation(single, PP))(order_keys)
    filled = jnp.take_along_axis(filled, orders, axis=1)
    filled = jnp.transpose(filled.reshape(N_QRY, N_DOC, PP), (1, 0, 2)).reshape(-1)
    return filled


def pattern_table(key):
    base_key = jax.random.fold_in(key, 7301)
    keys = jax.random.split(base_key, 2)
    entries = jax.random.randint(keys[0], (N_QRY, DEVICES), 0, 2)
    forced = jax.random.randint(keys[1], (N_QRY,), 0, DEVICES)
    return entries.at[jnp.arange(N_QRY), forced].set(1).astype(jnp.int32)


def passage_noise(key, row):
    row_key = jax.random.fold_in(jax.random.fold_in(key, 7101), row)
    values = jnp.clip(jax.random.normal(row_key, (D,), jnp.float32), -4.0, 4.0)
    return values


def draw_passages(key, part):
    rows = jnp.arange(NP, dtype=jnp.int32)
    noise = jax.vmap(lambda single: passage_noise(key, single))(rows)
    scales = jnp.exp(jax.random.uniform(jax.random.fold_in(key, 7103), (NP, 1), jnp.float32, math.log(0.6), math.log(2.5)))
    values = noise * scales
    return values.astype(jnp.bfloat16)


def draw_queries(key, part):
    keys = jax.random.split(jax.random.fold_in(key, 7201), 2)
    noise = jnp.clip(jax.random.normal(keys[0], (NQ, D), jnp.float32), -4.0, 4.0)
    scales = jnp.exp(jax.random.uniform(keys[1], (NQ, 1), jnp.float32, math.log(0.6), math.log(2.5)))
    values = noise * scales
    return values.astype(jnp.bfloat16)


def draw_passage_route(key, part):
    routes = route_table(key)
    return routes


def draw_pattern(key, part):
    return pattern_table(key)


def draw_teacher(key, part):
    keys = jax.random.split(jax.random.fold_in(key, 7401), 2)
    scales = jnp.exp(jax.random.uniform(keys[1], (NQ, 1), jnp.float32, math.log(0.5), math.log(5.0)))
    values = scales * jnp.clip(jax.random.normal(keys[0], (NQ, NDOC), jnp.float32), -4.0, 4.0)
    return values


def setup_inputs(seed: int = 0) -> dict:
    arg_keys = jax.random.split(jax.random.key(seed), 6)
    return {
        "queries": draw_queries(jax.random.fold_in(arg_keys[5], 71), 0),
        "passages": draw_passages(jax.random.fold_in(arg_keys[5], 71), 0),
        "passage_route": draw_passage_route(jax.random.fold_in(arg_keys[5], 71), 0),
        "pattern": draw_pattern(jax.random.fold_in(arg_keys[5], 71), 0),
        "teacher": draw_teacher(jax.random.fold_in(arg_keys[5], 71), 0),
    }


score_scale = 0.03125
very_negative = -1.0e30


def reference(queries, passages, passage_route, pattern, teacher):
    n_queries = queries.shape[0]
    n_docs = teacher.shape[1]
    n_passages = passages.shape[0]
    scores = lax.dot_general(queries, passages, (((1,), (1,)), ((), ())), preferred_element_type=jnp.float32) * score_scale
    inverse = jnp.full((n_docs * MAXP,), n_passages, jnp.int32).at[passage_route.astype(jnp.int32)].set(jnp.arange(n_passages, dtype=jnp.int32))
    inverse_blocks = inverse.reshape(n_docs // DOC_DEV, DOC_DEV * MAXP)

    def pool_owner(indices):
        picked = jnp.take(scores, indices, axis=1, mode="fill", fill_value=very_negative)
        masked = jnp.where((indices < n_passages)[None, :], picked, very_negative)
        masked = masked.reshape(n_queries, DOC_DEV, MAXP)
        highest = jnp.max(masked, axis=2)
        return highest + jnp.log(jnp.sum(jnp.exp(masked - highest[:, :, None]), axis=2))

    blocks = lax.map(pool_owner, inverse_blocks)
    pooled = jnp.transpose(blocks, (1, 0, 2)).reshape(n_queries, n_docs)
    active = jnp.repeat(jnp.repeat(pattern, QRY_DEV, axis=0), DOC_DEV, axis=1) > 0
    doc_scores = jnp.where(active, pooled, jnp.float32(0.0))
    peak_student = jnp.max(jnp.where(active, pooled, very_negative), axis=1)
    student_total = peak_student + jnp.log(jnp.sum(jnp.where(active, jnp.exp(pooled - peak_student[:, None]), jnp.float32(0.0)), axis=1))
    peak_teacher = jnp.max(jnp.where(active, teacher, very_negative), axis=1)
    teacher_total = peak_teacher + jnp.log(jnp.sum(jnp.where(active, jnp.exp(teacher - peak_teacher[:, None]), jnp.float32(0.0)), axis=1))
    probs = jnp.where(active, jnp.exp(teacher - teacher_total[:, None]), jnp.float32(0.0))
    divergence = jnp.sum(probs * (teacher - teacher_total[:, None] - pooled + student_total[:, None]), axis=1)
    return doc_scores, divergence
```

```python
import functools

import jax
import jax.numpy as jnp
from jax import lax
from jax.experimental import pallas as pl
from jax.experimental.pallas import tpu as pltpu
from jax.sharding import Mesh
from jax.sharding import PartitionSpec as P

MESH = pl.DeviceIdType.MESH
AXES = ("y", "z", "x", "c")
F32, BF16, I32 = jnp.float32, jnp.bfloat16, jnp.int32
SCALE = 0.03125
LOW = -1e30
CAP = 4
MAXP = 16


def mod(a, n):
    return lax.rem(a + 2 * n, n)


def kernel(
    ny, nz, nx,
    q_ref, p_ref, route_ref, pat_ref, teach_ref,
    docs_ref, div_ref,
    qall, pperm, send, recv, id_send, id_recv, doc_of, onehot, onehot_t, top,
    stat, stat_got, row, row_got,
    qs_sem, qr_sem, cs_sem, cr_sem, own_sem, ids_sem, idr_sem, ss_sem, sr_sem,
    xs_sem, xr_sem, ds_sem, dr_sem,
):
    y, z = lax.axis_index("y"), lax.axis_index("z")
    x, c = lax.axis_index("x"), lax.axis_index("c")
    ndoc, nqry = ny * nz, nx * 2
    me_doc, me_qry = y * nz + z, x * 2 + c
    right, left = mod(x + 1, nx), mod(x - 1, nx)
    npass = p_ref.shape[0]
    slots = ndoc * CAP

    barrier = pltpu.get_barrier_semaphore()

    def doc_peer(k):
        s = lax.div(k, ny)
        half = lax.div(s + 1, 2)
        dz = nz // 2 + jnp.where(lax.rem(s, 2) == 0, half, -half)
        return mod(y + lax.rem(k, ny), ny), mod(z + dz, nz)

    def each_doc_peer(body):
        def step(k, carry):
            py, pz = doc_peer(k)
            body(py, pz)
            return carry

        lax.fori_loop(0, ndoc - ny, step, 0)
        for dy in range(1, ny):
            body(mod(y + dy, ny), z)

    def each_qry_peer(body):
        def step(k, carry):
            peer = mod(me_qry + k, nqry)
            body(peer, lax.div(peer, 2), lax.rem(peer, 2))
            return carry

        lax.fori_loop(1, nqry, step, 0)

    each_qry_peer(
        lambda peer, px, pc: pl.semaphore_signal(
            barrier, inc=1, device_id={"x": px, "c": pc}, device_id_type=MESH
        )
    )
    each_doc_peer(
        lambda py, pz: pl.semaphore_signal(
            barrier, inc=1, device_id={"y": py, "z": pz}, device_id_type=MESH
        )
    )

    route = route_ref[...]
    target = lax.shift_right_logical(route, 8 + (nqry.bit_length() - 1))
    to = lax.broadcasted_iota(I32, (ndoc, npass), 0) == target
    tri = (
        lax.broadcasted_iota(I32, (npass, npass), 0) < lax.broadcasted_iota(I32, (npass, npass), 1)
    ).astype(F32).astype(BF16)
    ahead = jnp.dot(to.astype(F32).astype(BF16), tri, preferred_element_type=F32)
    rank = jnp.sum(jnp.where(to, ahead, 0.0), axis=0, keepdims=True).astype(I32)
    place = target * CAP + rank
    put = lax.broadcasted_iota(I32, (slots, npass), 0) == place
    put_b = put.astype(F32).astype(BF16)
    local = jnp.bitwise_and(route, 255) // MAXP + 1

    width = 512

    def permute(k, carry):
        cols = pl.ds(pl.multiple_of(k * width, width), width)
        pperm[:, cols] = jnp.dot(put_b, p_ref[:, cols], preferred_element_type=F32).astype(BF16)
        return carry

    lax.fori_loop(0, p_ref.shape[1] // width, permute, 0)

    owner_rows = lax.broadcasted_iota(I32, (ndoc, npass), 0)
    lane = lax.broadcasted_iota(I32, (ndoc, 128), 1)
    ids = jnp.zeros((ndoc, 128), F32)
    for j in range(CAP):
        hit = jnp.where(owner_rows * CAP + j == place, local.astype(F32), 0.0)
        ids = jnp.where(lax.rem(lane, CAP) == j, jnp.sum(hit, axis=1, keepdims=True), ids)
    id_send[...] = ids.reshape(ndoc, 1, 128)

    teach = teach_ref[...]
    t_top = jnp.max(teach, axis=0, keepdims=True)
    t_exp = jnp.exp(teach - t_top)
    t_sum = jnp.sum(t_exp, axis=0, keepdims=True)
    t_weight = t_exp / t_sum
    t_total = t_top + jnp.log(t_sum)
    group = me_doc * nqry + me_qry
    col = jnp.sum(
        jnp.where(lax.broadcasted_iota(I32, pat_ref.shape, 1) == group, pat_ref[...], 0).astype(F32),
        axis=1, keepdims=True,
    )
    nq = teach.shape[1]
    per = nq // nqry
    spread = lax.broadcasted_iota(I32, (nqry, nq), 1) // per == lax.broadcasted_iota(I32, (nqry, nq), 0)
    active = jnp.sum(jnp.where(spread, col, 0.0), axis=0, keepdims=True) > 0.5

    pl.semaphore_wait(barrier, ndoc - 1 + nqry - 1)

    half = q_ref.shape[0] // 2

    def rows_of(shard, h):
        return pl.ds(pl.multiple_of(shard * (2 * half) + h * half, half), half)

    def x_copy(src, shard, h, k, to_x):
        return pltpu.make_async_remote_copy(
            src_ref=src, dst_ref=qall.at[rows_of(shard, h)], send_sem=qs_sem.at[k], recv_sem=qr_sem.at[k],
            device_id={"x": to_x}, device_id_type=MESH,
        )

    def c_copy(src, rows, k):
        return pltpu.make_async_remote_copy(
            src_ref=src, dst_ref=qall.at[rows], send_sem=cs_sem.at[k], recv_sem=cr_sem.at[k],
            device_id={"c": 1 - c}, device_id_type=MESH,
        )

    sh_l, sh_r, sh_o = left * 2 + c, right * 2 + c, mod(x + 2, nx) * 2 + c
    own_rows = pl.ds(pl.multiple_of(me_qry * (2 * half), 2 * half), 2 * half)
    sends = [
        x_copy(q_ref.at[pl.ds(0, half)], me_qry, 0, 0, right),
        x_copy(q_ref.at[pl.ds(half, half)], me_qry, 1, 3, left),
        x_copy(q_ref.at[pl.ds(half, half)], me_qry, 1, 1, right),
        x_copy(q_ref.at[pl.ds(0, half)], me_qry, 0, 4, left),
        c_copy(q_ref, own_rows, 0),
    ]
    for s in sends:
        s.start()
    keep = pltpu.make_async_copy(q_ref, qall.at[own_rows], own_sem)
    keep.start()

    def send_id(py, pz):
        pltpu.make_async_remote_copy(
            src_ref=id_send.at[py * nz + pz], dst_ref=id_recv.at[me_doc], send_sem=ids_sem, recv_sem=idr_sem,
            device_id={"y": py, "z": pz}, device_id_type=MESH,
        ).start()

    each_doc_peer(send_id)
    id_recv[me_doc] = id_send[me_doc]

    for k, shard, h in ((0, sh_l, 0), (3, sh_r, 1), (1, sh_l, 1), (4, sh_r, 0), (2, sh_o, 0), (5, sh_o, 1)):
        rows = rows_of(shard, h)
        x_copy(qall.at[rows], shard, h, k, right).wait_recv()
        if k == 0:
            relay = x_copy(qall.at[rows], shard, h, 2, right)
            relay.start()
            sends.append(relay)
        if k == 3:
            relay = x_copy(qall.at[rows], shard, h, 5, left)
            relay.start()
            sends.append(relay)
        over = c_copy(qall.at[rows], rows, k + 1)
        over.start()
        sends.append(over)

    pltpu.make_async_copy(id_recv.at[pl.ds(0, ndoc - 1)], id_recv.at[pl.ds(0, ndoc - 1)], idr_sem).wait()
    pltpu.make_async_copy(id_send.at[pl.ds(0, ndoc - 1)], id_send.at[pl.ds(0, ndoc - 1)], ids_sem).wait()
    got = id_recv[...].reshape(ndoc, 128).astype(BF16)
    grow = ndoc * 8
    wide = (
        lax.broadcasted_iota(I32, (grow, ndoc), 0) // 8 == lax.broadcasted_iota(I32, (grow, ndoc), 1)
    ).astype(F32).astype(BF16)
    lines = jnp.dot(wide, got, preferred_element_type=F32)
    r_i = lax.broadcasted_iota(I32, (grow, 128), 0)
    l_i = lax.broadcasted_iota(I32, (grow, 128), 1)
    mine = jnp.sum(jnp.where(lax.rem(r_i, 8) == l_i, lines, 0.0), axis=1, keepdims=True)
    doc = jnp.broadcast_to(mine, (grow, 128)).astype(I32) - 1
    doc_of[...] = doc.reshape(ndoc, 8, 128)
    code = jnp.where(doc >= 0, doc + MAXP * (lax.rem(r_i, 8) // CAP), -1)
    hot = (code == l_i).astype(F32)
    onehot[...] = hot.astype(BF16)
    onehot_t[...] = hot.T.astype(BF16)

    keep.wait()
    c_copy(q_ref, own_rows, 0).wait_recv()
    partner = 1 - c
    for k, sh, h in ((0, left, 0), (3, right, 1), (1, left, 1), (4, right, 0), (2, mod(x + 2, nx), 0), (5, mod(x + 2, nx), 1)):
        rows = rows_of(sh * 2 + partner, h)
        c_copy(qall.at[rows], rows, k + 1).wait_recv()
    for s in sends:
        s.wait_send()

    scores = lax.dot_general(
        pperm[...], qall[...], (((1,), (1,)), ((), ())), preferred_element_type=F32
    ) * SCALE
    lo = scores[:, :128].reshape(ndoc // 2, 8, 128)
    hi = scores[:, 128:].reshape(ndoc // 2, 8, 128)
    front = lax.broadcasted_iota(I32, (ndoc // 2, 8, 128), 1) < CAP
    even = jnp.where(front, lo, pltpu.roll(hi, CAP, 1))
    odd = jnp.where(front, pltpu.roll(lo, CAP, 1), hi)
    send[:, 0] = even
    send[:, 1] = odd

    def send_scores(py, pz):
        d = py * nz + pz
        pltpu.make_async_remote_copy(
            src_ref=send.at[lax.div(d, 2), lax.rem(d, 2)], dst_ref=recv.at[me_doc], send_sem=ss_sem,
            recv_sem=sr_sem, device_id={"y": py, "z": pz}, device_id_type=MESH,
        ).start()

    each_doc_peer(send_scores)
    recv[me_doc] = send[lax.div(me_doc, 2), lax.rem(me_doc, 2)]
    pltpu.make_async_copy(recv.at[pl.ds(0, ndoc - 1)], recv.at[pl.ds(0, ndoc - 1)], sr_sem).wait()

    def tops(s, best):
        val, d = recv[s], doc_of[s]
        return tuple(jnp.maximum(b, jnp.where(d == t, val, LOW)) for t, b in enumerate(best))

    best = lax.fori_loop(0, ndoc, tops, tuple(jnp.full((8, 128), LOW, F32) for _ in range(MAXP)))
    for t in range(MAXP):
        top[t : t + 1] = jnp.max(best[t][:CAP], axis=0, keepdims=True)
        top[MAXP + t : MAXP + t + 1] = jnp.max(best[t][CAP:], axis=0, keepdims=True)
    top_b = top[...].astype(BF16)
    pad = jnp.zeros((128 - 2 * MAXP, 128), BF16)
    of_row = jnp.dot(onehot[...], jnp.concatenate([top_b, pad], axis=0), preferred_element_type=F32)
    e = jnp.exp(recv[...].reshape(grow, 128) - of_row)
    e_hi = e.astype(BF16)
    e_lo = (e - e_hi.astype(F32)).astype(BF16)
    total = jnp.dot(onehot_t[...], e_hi, preferred_element_type=F32) + jnp.dot(
        onehot_t[...], e_lo, preferred_element_type=F32
    )
    lse = top_b.astype(F32) + jnp.log(total[: 2 * MAXP])
    pooled = jnp.concatenate([lse[:MAXP], lse[MAXP:]], axis=1)
    docs_ref[...] = jnp.where(active, pooled, 0.0)

    s_top = jnp.max(pooled, axis=0, keepdims=True)
    s_total = s_top + jnp.log(jnp.sum(jnp.exp(pooled - s_top), axis=0, keepdims=True))
    mean = jnp.sum(t_weight * (teach - pooled), axis=0, keepdims=True)
    s_total = jnp.where(active, s_total, LOW)
    t_tot = jnp.where(active, t_total, LOW)
    mean = jnp.where(active, mean, 0.0)
    fill = jnp.zeros((5, nq), F32)
    stats = jnp.concatenate([s_total, t_tot, mean, fill], axis=0)
    stat[0] = stats[:, :128]
    stat[1] = stats[:, 128:]

    def send_stat(peer, px, pc):
        pltpu.make_async_remote_copy(
            src_ref=stat.at[lax.div(peer * per, 128)], dst_ref=stat_got.at[me_qry], send_sem=xs_sem,
            recv_sem=xr_sem, device_id={"x": px, "c": pc}, device_id_type=MESH,
        ).start()

    each_qry_peer(send_stat)
    stat_got[me_qry] = stat[lax.div(me_qry * per, 128)]
    pltpu.make_async_copy(stat_got.at[pl.ds(0, nqry - 1)], stat_got.at[pl.ds(0, nqry - 1)], xr_sem).wait()
    part = stat_got[...]
    peak = jnp.max(part, axis=0)
    mass = jnp.exp(part - peak[None])
    summed = jnp.sum(mass, axis=0)
    totals = peak + jnp.log(summed)
    mean8 = jnp.sum(mass[:, 1:2] * part[:, 2:3], axis=0) / summed[1:2]
    shift = lax.rem(me_qry * per, 128)
    back = mod(-shift, 128)
    lane1 = lax.broadcasted_iota(I32, (1, 128), 1)
    r0 = pltpu.roll(totals[0:1], back, 1)
    r1 = pltpu.roll(totals[1:2], lax.rem(back + per, 128), 1)
    r2 = pltpu.roll(mean8, lax.rem(back + 2 * per, 128), 1)
    line = jnp.where(lane1 < per, r0, jnp.where(lane1 < 2 * per, r1, r2))
    row[...] = line
    row_got[me_doc] = line

    def send_row(py, pz):
        pltpu.make_async_remote_copy(
            src_ref=row, dst_ref=row_got.at[me_doc], send_sem=ds_sem, recv_sem=dr_sem,
            device_id={"y": py, "z": pz}, device_id_type=MESH,
        ).start()

    each_doc_peer(send_row)
    pltpu.make_async_copy(row_got.at[pl.ds(0, ndoc - 1)], row_got.at[pl.ds(0, ndoc - 1)], dr_sem).wait()
    rows = row_got[...].reshape(ndoc, 128)
    peak = jnp.max(rows, axis=0, keepdims=True)
    mass = jnp.exp(rows - peak)
    summed = jnp.sum(mass, axis=0, keepdims=True)
    totals = peak + jnp.log(summed)
    weighted = jnp.sum(pltpu.roll(mass, per, 1) * rows, axis=0, keepdims=True)
    at2 = weighted / pltpu.roll(summed, per, 1)
    out = pltpu.roll(at2, 128 - 2 * per, 1) - pltpu.roll(totals, 128 - per, 1) + totals
    div_ref[...] = out[:, :per]

    pltpu.make_async_copy(recv.at[pl.ds(0, ndoc - 1)], recv.at[pl.ds(0, ndoc - 1)], ss_sem).wait()
    pltpu.make_async_copy(stat_got.at[pl.ds(0, nqry - 1)], stat_got.at[pl.ds(0, nqry - 1)], xs_sem).wait()
    pltpu.make_async_copy(row_got.at[pl.ds(0, ndoc - 1)], row_got.at[pl.ds(0, ndoc - 1)], ds_sem).wait()


def on_device(ny, nz, nx, queries, passages, route, pattern, teacher):
    ndoc, nqry = ny * nz, nx * 2
    npass, dim = passages.shape
    rows_dev = queries.shape[0]
    nq, docs = teacher.shape
    vmem = pl.BlockSpec(memory_space=pltpu.VMEM)
    dma = pltpu.SemaphoreType.DMA
    pooled, divergence = pl.pallas_call(
        functools.partial(kernel, ny, nz, nx),
        out_shape=(
            jax.ShapeDtypeStruct((docs, nq), F32),
            jax.ShapeDtypeStruct((1, rows_dev), F32),
        ),
        in_specs=[vmem] * 5,
        out_specs=(vmem, vmem),
        scratch_shapes=[
            pltpu.VMEM((nq, dim), BF16),
            pltpu.VMEM((ndoc * CAP, dim), BF16),
            pltpu.VMEM((ndoc // 2, 2, 8, 128), F32),
            pltpu.VMEM((ndoc, 8, 128), F32),
            pltpu.VMEM((ndoc, 1, 128), F32),
            pltpu.VMEM((ndoc, 1, 128), F32),
            pltpu.VMEM((ndoc, 8, 128), I32),
            pltpu.VMEM((ndoc * 8, 128), BF16),
            pltpu.VMEM((128, ndoc * 8), BF16),
            pltpu.VMEM((2 * MAXP, 128), F32),
            pltpu.VMEM((2, 8, 128), F32),
            pltpu.VMEM((nqry, 8, 128), F32),
            pltpu.VMEM((1, 128), F32),
            pltpu.VMEM((ndoc, 1, 128), F32),
            dma((6,)), dma((6,)), dma((7,)), dma((7,)),
            dma, dma, dma, dma, dma, dma, dma, dma, dma,
        ],
        compiler_params=pltpu.CompilerParams(
            collective_id=0, has_side_effects=True, vmem_limit_bytes=48 * 1024 * 1024
        ),
    )(queries, passages, route.reshape(1, npass), pattern, teacher.T)
    return pooled.T, divergence.reshape(rows_dev)


def solution(mesh):
    split = Mesh(mesh.devices.reshape(4, -1, 4, 2), AXES)
    ny, nz, nx = (split.shape[a] for a in ("y", "z", "x"))
    placed = (P(("x", "c"), None), P(AXES, None), P(AXES), P(), P(None, AXES))
    return jax.shard_map(
        functools.partial(on_device, ny, nz, nx),
        mesh=split,
        in_specs=placed,
        out_specs=(P(None, AXES), P(("x", "c"))),
        check_vma=False,
    )
```

```python
import functools

import jax
import jax.numpy as jnp
from jax import lax
from jax.experimental import pallas as pl
from jax.experimental.pallas import tpu as pltpu
from jax.sharding import Mesh
from jax.sharding import PartitionSpec as P

MESH = pl.DeviceIdType.MESH
AXES = ("y", "z", "x", "c")
F32, BF16, I32 = jnp.float32, jnp.bfloat16, jnp.int32
SCALE = 0.03125
LOW = -1e30
CAP = 4
MAXP = 16


def mod(a, n):
    return lax.rem(a + 2 * n, n)


def kernel(
    ny, nz, nx,
    q_ref, p_hbm, route_hbm, pat_hbm, teach_hbm,
    docs_ref, div_ref,
    p_ref, route_ref, pat_ref, teach_ref, qall, pperm, send, recv, id_send, id_recv, doc_of, onehot, onehot_t, top,
    stat, stat_got, row, row_got,
    in_sem, z2_sem, z4_sem, y_sem, qs_sem, qr_sem, cs_sem, cr_sem, ids_sem, idr_sem, ss_sem, sr_sem,
    xs_sem, xr_sem, ds_sem, dr_sem,
):
    y, z = lax.axis_index("y"), lax.axis_index("z")
    x, c = lax.axis_index("x"), lax.axis_index("c")
    ndoc, nqry = ny * nz, nx * 2
    me_doc, me_qry = y * nz + z, x * 2 + c
    right, left = mod(x + 1, nx), mod(x - 1, nx)
    npass = p_hbm.shape[0]
    slots = ndoc * CAP

    barrier = pltpu.get_barrier_semaphore()

    def doc_peer(k):
        s = lax.div(k, ny)
        half = lax.div(s + 1, 2)
        dz = nz // 2 + jnp.where(lax.rem(s, 2) == 0, half, -half)
        return mod(y + lax.rem(k, ny), ny), mod(z + dz, nz)

    def each_doc_peer(body):
        def step(k, carry):
            py, pz = doc_peer(k)
            body(py, pz)
            return carry

        lax.fori_loop(0, ndoc - ny, step, 0)
        for dy in range(1, ny):
            body(mod(y + dy, ny), z)

    def each_qry_peer(body):
        def step(k, carry):
            peer = mod(me_qry + k, nqry)
            body(peer, lax.div(peer, 2), lax.rem(peer, 2))
            return carry

        lax.fori_loop(1, nqry, step, 0)

    half = q_ref.shape[0] // 2
    own_rows = pl.ds(pl.multiple_of(me_qry * (2 * half), 2 * half), 2 * half)
    loads = [
        pltpu.make_async_copy(src, dst, in_sem.at[k])
        for k, (src, dst) in enumerate((
            (route_hbm, route_ref), (p_hbm, p_ref), (teach_hbm, teach_ref), (pat_hbm, pat_ref),
            (q_ref, qall.at[own_rows]),
        ))
    ]
    for load in loads:
        load.start()

    def tell(sem, **to):
        pl.semaphore_signal(sem, inc=1, device_id=to, device_id_type=MESH)

    tell(barrier, x=right)
    tell(barrier, x=left)
    tell(barrier, c=1 - c)
    for k in (1, -1, 2, -2):
        tell(barrier, z=mod(z + k, nz))
    for k in range(1, ny):
        tell(barrier, y=mod(y + k, ny))
    pl.semaphore_wait(barrier, 7 + ny - 1)


    def rows_of(shard, h):
        return pl.ds(pl.multiple_of(shard * (2 * half) + h * half, half), half)

    def x_copy(src, shard, h, k, to_x):
        return pltpu.make_async_remote_copy(
            src_ref=src, dst_ref=qall.at[rows_of(shard, h)], send_sem=qs_sem.at[k], recv_sem=qr_sem.at[k],
            device_id={"x": to_x}, device_id_type=MESH,
        )

    def c_copy(src, rows, k):
        return pltpu.make_async_remote_copy(
            src_ref=src, dst_ref=qall.at[rows], send_sem=cs_sem.at[k], recv_sem=cr_sem.at[k],
            device_id={"c": 1 - c}, device_id_type=MESH,
        )

    sh_l, sh_r, sh_o = left * 2 + c, right * 2 + c, mod(x + 2, nx) * 2 + c
    sends = [
        x_copy(q_ref.at[pl.ds(0, half)], me_qry, 0, 0, right),
        x_copy(q_ref.at[pl.ds(half, half)], me_qry, 1, 3, left),
        x_copy(q_ref.at[pl.ds(half, half)], me_qry, 1, 1, right),
        x_copy(q_ref.at[pl.ds(0, half)], me_qry, 0, 4, left),
        c_copy(q_ref, own_rows, 0),
    ]
    for s in sends:
        s.start()

    def tell_z(sem, far):
        tell(sem, z=mod(z + far, nz))
        tell(sem, z=mod(z - far, nz))

    def collect(pieces):
        for k, shard, h in pieces:
            rows = rows_of(shard, h)
            x_copy(qall.at[rows], shard, h, k, right).wait_recv()
            if k == 0:
                relay = x_copy(qall.at[rows], shard, h, 2, right)
                relay.start()
                sends.append(relay)
            if k == 3:
                relay = x_copy(qall.at[rows], shard, h, 5, left)
                relay.start()
                sends.append(relay)
            over = c_copy(qall.at[rows], rows, k + 1)
            over.start()
            sends.append(over)

    tell_z(z2_sem, 2)

    loads[0].wait()
    route = route_ref[...]
    target = lax.shift_right_logical(route, 8 + (nqry.bit_length() - 1))
    to = lax.broadcasted_iota(I32, (ndoc, npass), 0) == target
    tri = (
        lax.broadcasted_iota(I32, (npass, npass), 0) < lax.broadcasted_iota(I32, (npass, npass), 1)
    ).astype(F32).astype(BF16)
    ahead = jnp.dot(to.astype(F32).astype(BF16), tri, preferred_element_type=F32)
    rank = jnp.sum(jnp.where(to, ahead, 0.0), axis=0, keepdims=True).astype(I32)
    place = target * CAP + rank
    put = lax.broadcasted_iota(I32, (slots, npass), 0) == place
    put_b = put.astype(F32).astype(BF16)
    local = jnp.bitwise_and(route, 255) // MAXP + 1

    width = 512

    def permute(k, carry):
        cols = pl.ds(pl.multiple_of(k * width, width), width)
        pperm[:, cols] = jnp.dot(put_b, p_ref[:, cols], preferred_element_type=F32).astype(BF16)
        return carry

    loads[1].wait()
    chunks = p_ref.shape[1] // width
    pl.semaphore_wait(z2_sem, 2)
    tell_z(z4_sem, 4)
    lax.fori_loop(0, chunks // 2, permute, 0)
    pl.semaphore_wait(z4_sem, 2)
    for k in range(1, ny):
        tell(y_sem, y=mod(y + k, ny))
    lax.fori_loop(chunks // 2, chunks, permute, 0)
    collect(((0, sh_l, 0), (3, sh_r, 1)))
    pl.semaphore_wait(y_sem, ny - 1)

    owner_rows = lax.broadcasted_iota(I32, (ndoc, npass), 0)
    lane = lax.broadcasted_iota(I32, (ndoc, 128), 1)
    ids = jnp.zeros((ndoc, 128), F32)
    for j in range(CAP):
        hit = jnp.where(owner_rows * CAP + j == place, local.astype(F32), 0.0)
        ids = jnp.where(lax.rem(lane, CAP) == j, jnp.sum(hit, axis=1, keepdims=True), ids)
    id_send[...] = ids.reshape(ndoc, 1, 128)

    def send_id(py, pz):
        pltpu.make_async_remote_copy(
            src_ref=id_send.at[py * nz + pz], dst_ref=id_recv.at[me_doc], send_sem=ids_sem, recv_sem=idr_sem,
            device_id={"y": py, "z": pz}, device_id_type=MESH,
        ).start()

    each_doc_peer(send_id)
    id_recv[me_doc] = id_send[me_doc]

    collect(((1, sh_l, 1), (4, sh_r, 0), (2, sh_o, 0), (5, sh_o, 1)))

    loads[4].wait()
    c_copy(q_ref, own_rows, 0).wait_recv()
    partner = 1 - c
    for k, sh, h in ((0, left, 0), (3, right, 1), (1, left, 1), (4, right, 0), (2, mod(x + 2, nx), 0), (5, mod(x + 2, nx), 1)):
        rows = rows_of(sh * 2 + partner, h)
        c_copy(qall.at[rows], rows, k + 1).wait_recv()
    for s in sends:
        s.wait_send()

    scores = lax.dot_general(
        pperm[...], qall[...], (((1,), (1,)), ((), ())), preferred_element_type=F32
    ) * SCALE
    lo = scores[:, :128].reshape(ndoc // 2, 8, 128)
    hi = scores[:, 128:].reshape(ndoc // 2, 8, 128)
    front = lax.broadcasted_iota(I32, (ndoc // 2, 8, 128), 1) < CAP
    even = jnp.where(front, lo, pltpu.roll(hi, CAP, 1))
    odd = jnp.where(front, pltpu.roll(lo, CAP, 1), hi)
    send[:, 0] = even
    send[:, 1] = odd

    def send_scores(py, pz):
        d = py * nz + pz
        pltpu.make_async_remote_copy(
            src_ref=send.at[lax.div(d, 2), lax.rem(d, 2)], dst_ref=recv.at[me_doc], send_sem=ss_sem,
            recv_sem=sr_sem, device_id={"y": py, "z": pz}, device_id_type=MESH,
        ).start()

    each_doc_peer(send_scores)
    recv[me_doc] = send[lax.div(me_doc, 2), lax.rem(me_doc, 2)]

    loads[2].wait()
    loads[3].wait()
    teach = teach_ref[...]
    t_top = jnp.max(teach, axis=0, keepdims=True)
    t_exp = jnp.exp(teach - t_top)
    t_sum = jnp.sum(t_exp, axis=0, keepdims=True)
    t_weight = t_exp / t_sum
    t_total = t_top + jnp.log(t_sum)
    group = me_doc * nqry + me_qry
    col = jnp.sum(
        jnp.where(lax.broadcasted_iota(I32, pat_ref.shape, 1) == group, pat_ref[...], 0).astype(F32),
        axis=1, keepdims=True,
    )
    nq = teach.shape[1]
    per = nq // nqry
    spread = lax.broadcasted_iota(I32, (nqry, nq), 1) // per == lax.broadcasted_iota(I32, (nqry, nq), 0)
    active = jnp.sum(jnp.where(spread, col, 0.0), axis=0, keepdims=True) > 0.5

    pltpu.make_async_copy(id_recv.at[pl.ds(0, ndoc - 1)], id_recv.at[pl.ds(0, ndoc - 1)], idr_sem).wait()
    pltpu.make_async_copy(id_send.at[pl.ds(0, ndoc - 1)], id_send.at[pl.ds(0, ndoc - 1)], ids_sem).wait()
    got = id_recv[...].reshape(ndoc, 128).astype(BF16)
    grow = ndoc * 8
    wide = (
        lax.broadcasted_iota(I32, (grow, ndoc), 0) // 8 == lax.broadcasted_iota(I32, (grow, ndoc), 1)
    ).astype(F32).astype(BF16)
    lines = jnp.dot(wide, got, preferred_element_type=F32)
    r_i = lax.broadcasted_iota(I32, (grow, 128), 0)
    l_i = lax.broadcasted_iota(I32, (grow, 128), 1)
    mine = jnp.sum(jnp.where(lax.rem(r_i, 8) == l_i, lines, 0.0), axis=1, keepdims=True)
    doc = jnp.broadcast_to(mine, (grow, 128)).astype(I32) - 1
    doc_of[...] = doc.reshape(ndoc, 8, 128)
    code = jnp.where(doc >= 0, doc + MAXP * (lax.rem(r_i, 8) // CAP), -1)
    hot = (code == l_i).astype(F32)
    onehot[...] = hot.astype(BF16)
    onehot_t[...] = hot.T.astype(BF16)

    pltpu.make_async_copy(recv.at[pl.ds(0, ndoc - 1)], recv.at[pl.ds(0, ndoc - 1)], sr_sem).wait()

    def tops(s, best):
        val, d = recv[s], doc_of[s]
        return tuple(jnp.maximum(b, jnp.where(d == t, val, LOW)) for t, b in enumerate(best))

    best = lax.fori_loop(0, ndoc, tops, tuple(jnp.full((8, 128), LOW, F32) for _ in range(MAXP)))
    for t in range(MAXP):
        top[t : t + 1] = jnp.max(best[t][:CAP], axis=0, keepdims=True)
        top[MAXP + t : MAXP + t + 1] = jnp.max(best[t][CAP:], axis=0, keepdims=True)
    top_b = top[...].astype(BF16)
    pad = jnp.zeros((128 - 2 * MAXP, 128), BF16)
    of_row = jnp.dot(onehot[...], jnp.concatenate([top_b, pad], axis=0), preferred_element_type=F32)
    e = jnp.exp(recv[...].reshape(grow, 128) - of_row)
    e_hi = e.astype(BF16)
    e_lo = (e - e_hi.astype(F32)).astype(BF16)
    total = jnp.dot(onehot_t[...], e_hi, preferred_element_type=F32) + jnp.dot(
        onehot_t[...], e_lo, preferred_element_type=F32
    )
    lse = top_b.astype(F32) + jnp.log(total[: 2 * MAXP])
    pooled = jnp.concatenate([lse[:MAXP], lse[MAXP:]], axis=1)
    docs_ref[...] = jnp.where(active, pooled, 0.0)

    s_top = jnp.max(pooled, axis=0, keepdims=True)
    s_total = s_top + jnp.log(jnp.sum(jnp.exp(pooled - s_top), axis=0, keepdims=True))
    mean = jnp.sum(t_weight * (teach - pooled), axis=0, keepdims=True)
    s_total = jnp.where(active, s_total, LOW)
    t_tot = jnp.where(active, t_total, LOW)
    mean = jnp.where(active, mean, 0.0)
    fill = jnp.zeros((5, nq), F32)
    stats = jnp.concatenate([s_total, t_tot, mean, fill], axis=0)
    stat[0] = stats[:, :128]
    stat[1] = stats[:, 128:]

    def send_stat(peer, px, pc):
        pltpu.make_async_remote_copy(
            src_ref=stat.at[lax.div(peer * per, 128)], dst_ref=stat_got.at[me_qry], send_sem=xs_sem,
            recv_sem=xr_sem, device_id={"x": px, "c": pc}, device_id_type=MESH,
        ).start()

    each_qry_peer(send_stat)
    stat_got[me_qry] = stat[lax.div(me_qry * per, 128)]
    pltpu.make_async_copy(stat_got.at[pl.ds(0, nqry - 1)], stat_got.at[pl.ds(0, nqry - 1)], xr_sem).wait()
    part = stat_got[...]
    peak = jnp.max(part, axis=0)
    mass = jnp.exp(part - peak[None])
    summed = jnp.sum(mass, axis=0)
    totals = peak + jnp.log(summed)
    mean8 = jnp.sum(mass[:, 1:2] * part[:, 2:3], axis=0) / summed[1:2]
    shift = lax.rem(me_qry * per, 128)
    turn = mod(-shift, 128)
    lane1 = lax.broadcasted_iota(I32, (1, 128), 1)
    r0 = pltpu.roll(totals[0:1], turn, 1)
    r1 = pltpu.roll(totals[1:2], lax.rem(turn + per, 128), 1)
    r2 = pltpu.roll(mean8, lax.rem(turn + 2 * per, 128), 1)
    line = jnp.where(lane1 < per, r0, jnp.where(lane1 < 2 * per, r1, r2))
    row[...] = line
    row_got[me_doc] = line

    def send_row(py, pz):
        pltpu.make_async_remote_copy(
            src_ref=row, dst_ref=row_got.at[me_doc], send_sem=ds_sem, recv_sem=dr_sem,
            device_id={"y": py, "z": pz}, device_id_type=MESH,
        ).start()

    each_doc_peer(send_row)
    pltpu.make_async_copy(row_got.at[pl.ds(0, ndoc - 1)], row_got.at[pl.ds(0, ndoc - 1)], dr_sem).wait()
    rows = row_got[...].reshape(ndoc, 128)
    peak = jnp.max(rows, axis=0, keepdims=True)
    mass = jnp.exp(rows - peak)
    summed = jnp.sum(mass, axis=0, keepdims=True)
    totals = peak + jnp.log(summed)
    weighted = jnp.sum(pltpu.roll(mass, per, 1) * rows, axis=0, keepdims=True)
    at2 = weighted / pltpu.roll(summed, per, 1)
    out = pltpu.roll(at2, 128 - 2 * per, 1) - pltpu.roll(totals, 128 - per, 1) + totals
    div_ref[...] = out[:, :per]

    pltpu.make_async_copy(recv.at[pl.ds(0, ndoc - 1)], recv.at[pl.ds(0, ndoc - 1)], ss_sem).wait()
    pltpu.make_async_copy(stat_got.at[pl.ds(0, nqry - 1)], stat_got.at[pl.ds(0, nqry - 1)], xs_sem).wait()
    pltpu.make_async_copy(row_got.at[pl.ds(0, ndoc - 1)], row_got.at[pl.ds(0, ndoc - 1)], ds_sem).wait()


def on_device(ny, nz, nx, queries, passages, route, pattern, teacher):
    ndoc, nqry = ny * nz, nx * 2
    npass, dim = passages.shape
    rows_dev = queries.shape[0]
    nq, docs = teacher.shape
    vmem = pl.BlockSpec(memory_space=pltpu.VMEM)
    hbm = pl.BlockSpec(memory_space=pltpu.HBM)
    dma, regular = pltpu.SemaphoreType.DMA, pltpu.SemaphoreType.REGULAR
    pooled, divergence = pl.pallas_call(
        functools.partial(kernel, ny, nz, nx),
        out_shape=(
            jax.ShapeDtypeStruct((docs, nq), F32),
            jax.ShapeDtypeStruct((1, rows_dev), F32),
        ),
        in_specs=[hbm] * 5,
        out_specs=(vmem, vmem),
        scratch_shapes=[
            pltpu.VMEM((npass, dim), BF16),
            pltpu.VMEM((1, npass), I32),
            pltpu.VMEM(pattern.shape, I32),
            pltpu.VMEM((docs, nq), F32),
            pltpu.VMEM((nq, dim), BF16),
            pltpu.VMEM((ndoc * CAP, dim), BF16),
            pltpu.VMEM((ndoc // 2, 2, 8, 128), F32),
            pltpu.VMEM((ndoc, 8, 128), F32),
            pltpu.VMEM((ndoc, 1, 128), F32),
            pltpu.VMEM((ndoc, 1, 128), F32),
            pltpu.VMEM((ndoc, 8, 128), I32),
            pltpu.VMEM((ndoc * 8, 128), BF16),
            pltpu.VMEM((128, ndoc * 8), BF16),
            pltpu.VMEM((2 * MAXP, 128), F32),
            pltpu.VMEM((2, 8, 128), F32),
            pltpu.VMEM((nqry, 8, 128), F32),
            pltpu.VMEM((1, 128), F32),
            pltpu.VMEM((ndoc, 1, 128), F32),
            dma((5,)), regular, regular, regular,
            dma((6,)), dma((6,)), dma((7,)), dma((7,)),
            dma, dma, dma, dma, dma, dma, dma, dma,
        ],
        compiler_params=pltpu.CompilerParams(
            collective_id=0, has_side_effects=True, vmem_limit_bytes=60 * 1024 * 1024
        ),
    )(queries, passages, route.reshape(1, npass), pattern, teacher.T)
    return pooled.T, divergence.reshape(rows_dev)


def solution(mesh):
    split = Mesh(mesh.devices.reshape(4, -1, 4, 2), AXES)
    ny, nz, nx = (split.shape[a] for a in ("y", "z", "x"))
    placed = (P(("x", "c"), None), P(AXES, None), P(AXES), P(), P(None, AXES))
    return jax.shard_map(
        functools.partial(on_device, ny, nz, nx),
        mesh=split,
        in_specs=placed,
        out_specs=(P(None, AXES), P(("x", "c"))),
        check_vma=False,
    )
```

```python
import functools
import math

import jax
import jax.numpy as jnp
from jax import lax
from jax.experimental import pallas as pl
from jax.experimental.pallas import tpu as pltpu
from jax.sharding import Mesh
from jax.sharding import PartitionSpec as P

MESH = pl.DeviceIdType.MESH
AXES = ("y", "z", "x", "c")
F32, BF16, I32 = jnp.float32, jnp.bfloat16, jnp.int32
SCALE = 0.03125
LOW = -1e30
LIMIT = 14.0
TOP_CODE = 32767.0
CAP = 4
MAXP = 16


def mod(a, n):
    return lax.rem(a + 2 * n, n)


def kernel(
    ny, nz, nx,
    q_ref, p_hbm, route_hbm, pat_hbm, teach_hbm,
    docs_ref, div_ref,
    p_ref, route_ref, pat_ref, teach_ref, qall, pperm, send, recv, value, id_send, id_recv, doc_of, onehot, onehot_t, top,
    stat, stat_got, row, row_got,
    in_sem, z2_sem, z4_sem, y_sem, qs_sem, qr_sem, cs_sem, cr_sem, ids_sem, idr_sem, ss_sem, sr_sem,
    xs_sem, xr_sem, ds_sem, dr_sem,
):
    y, z = lax.axis_index("y"), lax.axis_index("z")
    x, c = lax.axis_index("x"), lax.axis_index("c")
    ndoc, nqry = ny * nz, nx * 2
    me_doc, me_qry = y * nz + z, x * 2 + c
    right, left = mod(x + 1, nx), mod(x - 1, nx)
    npass = p_hbm.shape[0]
    slots = ndoc * CAP

    barrier = pltpu.get_barrier_semaphore()

    def doc_peer(k):
        s = lax.div(k, ny)
        half = lax.div(s + 1, 2)
        dz = nz // 2 + jnp.where(lax.rem(s, 2) == 0, half, -half)
        return mod(y + lax.rem(k, ny), ny), mod(z + dz, nz)

    def each_doc_peer(body):
        def step(k, carry):
            py, pz = doc_peer(k)
            body(py, pz)
            return carry

        lax.fori_loop(0, ndoc - ny, step, 0)
        for dy in range(1, ny):
            body(mod(y + dy, ny), z)

    def each_qry_peer(body):
        def step(k, carry):
            peer = mod(me_qry + k, nqry)
            body(peer, lax.div(peer, 2), lax.rem(peer, 2))
            return carry

        lax.fori_loop(1, nqry, step, 0)

    half = q_ref.shape[0] // 2
    own_rows = pl.ds(pl.multiple_of(me_qry * (2 * half), 2 * half), 2 * half)
    loads = [
        pltpu.make_async_copy(src, dst, in_sem.at[k])
        for k, (src, dst) in enumerate((
            (route_hbm, route_ref), (p_hbm, p_ref), (teach_hbm, teach_ref), (pat_hbm, pat_ref),
            (q_ref, qall.at[own_rows]),
        ))
    ]
    for load in loads:
        load.start()

    def tell(sem, **to):
        pl.semaphore_signal(sem, inc=1, device_id=to, device_id_type=MESH)

    tell(barrier, x=right)
    tell(barrier, x=left)
    tell(barrier, c=1 - c)
    for k in (1, -1, 2, -2):
        tell(barrier, z=mod(z + k, nz))
    for k in range(1, ny):
        tell(barrier, y=mod(y + k, ny))
    pl.semaphore_wait(barrier, 7 + ny - 1)


    def rows_of(shard, h):
        return pl.ds(pl.multiple_of(shard * (2 * half) + h * half, half), half)

    def x_copy(src, shard, h, k, to_x):
        return pltpu.make_async_remote_copy(
            src_ref=src, dst_ref=qall.at[rows_of(shard, h)], send_sem=qs_sem.at[k], recv_sem=qr_sem.at[k],
            device_id={"x": to_x}, device_id_type=MESH,
        )

    def c_copy(src, rows, k):
        return pltpu.make_async_remote_copy(
            src_ref=src, dst_ref=qall.at[rows], send_sem=cs_sem.at[k], recv_sem=cr_sem.at[k],
            device_id={"c": 1 - c}, device_id_type=MESH,
        )

    sh_l, sh_r, sh_o = left * 2 + c, right * 2 + c, mod(x + 2, nx) * 2 + c
    sends = [
        x_copy(q_ref.at[pl.ds(0, half)], me_qry, 0, 0, right),
        x_copy(q_ref.at[pl.ds(half, half)], me_qry, 1, 3, left),
        x_copy(q_ref.at[pl.ds(half, half)], me_qry, 1, 1, right),
        x_copy(q_ref.at[pl.ds(0, half)], me_qry, 0, 4, left),
        c_copy(q_ref, own_rows, 0),
    ]
    for s in sends:
        s.start()

    def tell_z(sem, far):
        tell(sem, z=mod(z + far, nz))
        tell(sem, z=mod(z - far, nz))

    def collect(pieces):
        for k, shard, h in pieces:
            rows = rows_of(shard, h)
            x_copy(qall.at[rows], shard, h, k, right).wait_recv()
            if k == 0:
                relay = x_copy(qall.at[rows], shard, h, 2, right)
                relay.start()
                sends.append(relay)
            if k == 3:
                relay = x_copy(qall.at[rows], shard, h, 5, left)
                relay.start()
                sends.append(relay)
            over = c_copy(qall.at[rows], rows, k + 1)
            over.start()
            sends.append(over)

    tell_z(z2_sem, 2)

    loads[0].wait()
    route = route_ref[...]
    target = lax.shift_right_logical(route, 8 + (nqry.bit_length() - 1))
    to = lax.broadcasted_iota(I32, (ndoc, npass), 0) == target
    tri = (
        lax.broadcasted_iota(I32, (npass, npass), 0) < lax.broadcasted_iota(I32, (npass, npass), 1)
    ).astype(F32).astype(BF16)
    ahead = jnp.dot(to.astype(F32).astype(BF16), tri, preferred_element_type=F32)
    rank = jnp.sum(jnp.where(to, ahead, 0.0), axis=0, keepdims=True).astype(I32)
    place = target * CAP + rank
    put = lax.broadcasted_iota(I32, (slots, npass), 0) == place
    put_b = put.astype(F32).astype(BF16)
    local = jnp.bitwise_and(route, 255) // MAXP + 1

    width = 512

    def permute(k, carry):
        cols = pl.ds(pl.multiple_of(k * width, width), width)
        pperm[:, cols] = jnp.dot(put_b, p_ref[:, cols], preferred_element_type=F32).astype(BF16)
        return carry

    loads[1].wait()
    chunks = p_ref.shape[1] // width
    pl.semaphore_wait(z2_sem, 2)
    tell_z(z4_sem, 4)
    lax.fori_loop(0, chunks // 2, permute, 0)
    pl.semaphore_wait(z4_sem, 2)
    for k in range(1, ny):
        tell(y_sem, y=mod(y + k, ny))
    lax.fori_loop(chunks // 2, chunks, permute, 0)
    collect(((0, sh_l, 0), (3, sh_r, 1)))
    pl.semaphore_wait(y_sem, ny - 1)

    owner_rows = lax.broadcasted_iota(I32, (ndoc, npass), 0)
    lane = lax.broadcasted_iota(I32, (ndoc, 128), 1)
    ids = jnp.zeros((ndoc, 128), F32)
    for j in range(CAP):
        hit = jnp.where(owner_rows * CAP + j == place, local.astype(F32), 0.0)
        ids = jnp.where(lax.rem(lane, CAP) == j, jnp.sum(hit, axis=1, keepdims=True), ids)
    id_send[...] = ids.reshape(ndoc, 1, 128)

    def send_id(py, pz):
        pltpu.make_async_remote_copy(
            src_ref=id_send.at[py * nz + pz], dst_ref=id_recv.at[me_doc], send_sem=ids_sem, recv_sem=idr_sem,
            device_id={"y": py, "z": pz}, device_id_type=MESH,
        ).start()

    each_doc_peer(send_id)
    id_recv[me_doc] = id_send[me_doc]

    collect(((1, sh_l, 1), (4, sh_r, 0), (2, sh_o, 0), (5, sh_o, 1)))

    loads[4].wait()
    c_copy(q_ref, own_rows, 0).wait_recv()
    partner = 1 - c
    for k, sh, h in ((0, left, 0), (3, right, 1), (1, left, 1), (4, right, 0), (2, mod(x + 2, nx), 0), (5, mod(x + 2, nx), 1)):
        rows = rows_of(sh * 2 + partner, h)
        c_copy(qall.at[rows], rows, k + 1).wait_recv()
    for s in sends:
        s.wait_send()

    scores = lax.dot_general(
        pperm[...], qall[...], (((1,), (1,)), ((), ())), preferred_element_type=F32
    ) * SCALE
    steps = TOP_CODE / math.log(1.0 + 2.0 * LIMIT * LIMIT * SCALE * q_ref.shape[1])
    size = jnp.floor(jnp.log(1.0 + 2.0 * jnp.abs(scores)) * steps + 0.5)
    scores = jnp.where(scores < 0.0, -size, size)
    lo = scores[:, :128].reshape(ndoc // 2, 8, 128)
    hi = scores[:, 128:].reshape(ndoc // 2, 8, 128)
    front = lax.broadcasted_iota(I32, (ndoc // 2, 8, 128), 1) < CAP
    even = jnp.where(front, lo, pltpu.roll(hi, CAP, 1))
    odd = jnp.where(front, pltpu.roll(lo, CAP, 1), hi)
    send[:, 0] = even.astype(I32).astype(jnp.int16)
    send[:, 1] = odd.astype(I32).astype(jnp.int16)

    def send_scores(py, pz):
        d = py * nz + pz
        pltpu.make_async_remote_copy(
            src_ref=send.at[lax.div(d, 2), lax.rem(d, 2)], dst_ref=recv.at[me_doc], send_sem=ss_sem,
            recv_sem=sr_sem, device_id={"y": py, "z": pz}, device_id_type=MESH,
        ).start()

    each_doc_peer(send_scores)
    recv[me_doc] = send[lax.div(me_doc, 2), lax.rem(me_doc, 2)]

    loads[2].wait()
    loads[3].wait()
    teach = teach_ref[...]
    t_top = jnp.max(teach, axis=0, keepdims=True)
    t_exp = jnp.exp(teach - t_top)
    t_sum = jnp.sum(t_exp, axis=0, keepdims=True)
    t_weight = t_exp / t_sum
    t_total = t_top + jnp.log(t_sum)
    group = me_doc * nqry + me_qry
    col = jnp.sum(
        jnp.where(lax.broadcasted_iota(I32, pat_ref.shape, 1) == group, pat_ref[...], 0).astype(F32),
        axis=1, keepdims=True,
    )
    nq = teach.shape[1]
    per = nq // nqry
    spread = lax.broadcasted_iota(I32, (nqry, nq), 1) // per == lax.broadcasted_iota(I32, (nqry, nq), 0)
    active = jnp.sum(jnp.where(spread, col, 0.0), axis=0, keepdims=True) > 0.5

    pltpu.make_async_copy(id_recv.at[pl.ds(0, ndoc - 1)], id_recv.at[pl.ds(0, ndoc - 1)], idr_sem).wait()
    pltpu.make_async_copy(id_send.at[pl.ds(0, ndoc - 1)], id_send.at[pl.ds(0, ndoc - 1)], ids_sem).wait()
    got = id_recv[...].reshape(ndoc, 128).astype(BF16)
    grow = ndoc * 8
    wide = (
        lax.broadcasted_iota(I32, (grow, ndoc), 0) // 8 == lax.broadcasted_iota(I32, (grow, ndoc), 1)
    ).astype(F32).astype(BF16)
    lines = jnp.dot(wide, got, preferred_element_type=F32)
    r_i = lax.broadcasted_iota(I32, (grow, 128), 0)
    l_i = lax.broadcasted_iota(I32, (grow, 128), 1)
    mine = jnp.sum(jnp.where(lax.rem(r_i, 8) == l_i, lines, 0.0), axis=1, keepdims=True)
    doc = jnp.broadcast_to(mine, (grow, 128)).astype(I32) - 1
    doc_of[...] = doc.reshape(ndoc, 8, 128)
    code = jnp.where(doc >= 0, doc + MAXP * (lax.rem(r_i, 8) // CAP), -1)
    hot = (code == l_i).astype(F32)
    onehot[...] = hot.astype(BF16)
    onehot_t[...] = hot.T.astype(BF16)

    pltpu.make_async_copy(recv.at[pl.ds(0, ndoc - 1)], recv.at[pl.ds(0, ndoc - 1)], sr_sem).wait()

    def tops(s, best):
        got = recv[s].astype(I32).astype(F32)
        size = 0.5 * (jnp.exp(jnp.abs(got) / steps) - 1.0)
        val, d = jnp.where(got < 0.0, -size, size), doc_of[s]
        value[s] = val
        return tuple(jnp.maximum(b, jnp.where(d == t, val, LOW)) for t, b in enumerate(best))

    best = lax.fori_loop(0, ndoc, tops, tuple(jnp.full((8, 128), LOW, F32) for _ in range(MAXP)))
    for t in range(MAXP):
        top[t : t + 1] = jnp.max(best[t][:CAP], axis=0, keepdims=True)
        top[MAXP + t : MAXP + t + 1] = jnp.max(best[t][CAP:], axis=0, keepdims=True)
    top_b = top[...].astype(BF16)
    pad = jnp.zeros((128 - 2 * MAXP, 128), BF16)
    of_row = jnp.dot(onehot[...], jnp.concatenate([top_b, pad], axis=0), preferred_element_type=F32)
    e = jnp.exp(value[...].reshape(grow, 128) - of_row)
    e_hi = e.astype(BF16)
    e_lo = (e - e_hi.astype(F32)).astype(BF16)
    total = jnp.dot(onehot_t[...], e_hi, preferred_element_type=F32) + jnp.dot(
        onehot_t[...], e_lo, preferred_element_type=F32
    )
    lse = top_b.astype(F32) + jnp.log(total[: 2 * MAXP])
    pooled = jnp.concatenate([lse[:MAXP], lse[MAXP:]], axis=1)
    docs_ref[...] = jnp.where(active, pooled, 0.0)

    s_top = jnp.max(pooled, axis=0, keepdims=True)
    s_total = s_top + jnp.log(jnp.sum(jnp.exp(pooled - s_top), axis=0, keepdims=True))
    mean = jnp.sum(t_weight * (teach - pooled), axis=0, keepdims=True)
    s_total = jnp.where(active, s_total, LOW)
    t_tot = jnp.where(active, t_total, LOW)
    mean = jnp.where(active, mean, 0.0)
    fill = jnp.zeros((5, nq), F32)
    stats = jnp.concatenate([s_total, t_tot, mean, fill], axis=0)
    stat[0] = stats[:, :128]
    stat[1] = stats[:, 128:]

    def send_stat(peer, px, pc):
        pltpu.make_async_remote_copy(
            src_ref=stat.at[lax.div(peer * per, 128)], dst_ref=stat_got.at[me_qry], send_sem=xs_sem,
            recv_sem=xr_sem, device_id={"x": px, "c": pc}, device_id_type=MESH,
        ).start()

    each_qry_peer(send_stat)
    stat_got[me_qry] = stat[lax.div(me_qry * per, 128)]
    pltpu.make_async_copy(stat_got.at[pl.ds(0, nqry - 1)], stat_got.at[pl.ds(0, nqry - 1)], xr_sem).wait()
    part = stat_got[...]
    peak = jnp.max(part, axis=0)
    mass = jnp.exp(part - peak[None])
    summed = jnp.sum(mass, axis=0)
    totals = peak + jnp.log(summed)
    mean8 = jnp.sum(mass[:, 1:2] * part[:, 2:3], axis=0) / summed[1:2]
    shift = lax.rem(me_qry * per, 128)
    turn = mod(-shift, 128)
    lane1 = lax.broadcasted_iota(I32, (1, 128), 1)
    r0 = pltpu.roll(totals[0:1], turn, 1)
    r1 = pltpu.roll(totals[1:2], lax.rem(turn + per, 128), 1)
    r2 = pltpu.roll(mean8, lax.rem(turn + 2 * per, 128), 1)
    line = jnp.where(lane1 < per, r0, jnp.where(lane1 < 2 * per, r1, r2))
    row[...] = line
    row_got[me_doc] = line

    def send_row(py, pz):
        pltpu.make_async_remote_copy(
            src_ref=row, dst_ref=row_got.at[me_doc], send_sem=ds_sem, recv_sem=dr_sem,
            device_id={"y": py, "z": pz}, device_id_type=MESH,
        ).start()

    each_doc_peer(send_row)
    pltpu.make_async_copy(row_got.at[pl.ds(0, ndoc - 1)], row_got.at[pl.ds(0, ndoc - 1)], dr_sem).wait()
    rows = row_got[...].reshape(ndoc, 128)
    peak = jnp.max(rows, axis=0, keepdims=True)
    mass = jnp.exp(rows - peak)
    summed = jnp.sum(mass, axis=0, keepdims=True)
    totals = peak + jnp.log(summed)
    weighted = jnp.sum(pltpu.roll(mass, per, 1) * rows, axis=0, keepdims=True)
    at2 = weighted / pltpu.roll(summed, per, 1)
    out = pltpu.roll(at2, 128 - 2 * per, 1) - pltpu.roll(totals, 128 - per, 1) + totals
    div_ref[...] = out[:, :per]

    pltpu.make_async_copy(recv.at[pl.ds(0, ndoc - 1)], recv.at[pl.ds(0, ndoc - 1)], ss_sem).wait()
    pltpu.make_async_copy(stat_got.at[pl.ds(0, nqry - 1)], stat_got.at[pl.ds(0, nqry - 1)], xs_sem).wait()
    pltpu.make_async_copy(row_got.at[pl.ds(0, ndoc - 1)], row_got.at[pl.ds(0, ndoc - 1)], ds_sem).wait()


def on_device(ny, nz, nx, queries, passages, route, pattern, teacher):
    ndoc, nqry = ny * nz, nx * 2
    npass, dim = passages.shape
    rows_dev = queries.shape[0]
    nq, docs = teacher.shape
    vmem = pl.BlockSpec(memory_space=pltpu.VMEM)
    hbm = pl.BlockSpec(memory_space=pltpu.HBM)
    dma, regular = pltpu.SemaphoreType.DMA, pltpu.SemaphoreType.REGULAR
    pooled, divergence = pl.pallas_call(
        functools.partial(kernel, ny, nz, nx),
        out_shape=(
            jax.ShapeDtypeStruct((docs, nq), F32),
            jax.ShapeDtypeStruct((1, rows_dev), F32),
        ),
        in_specs=[hbm] * 5,
        out_specs=(vmem, vmem),
        scratch_shapes=[
            pltpu.VMEM((npass, dim), BF16),
            pltpu.VMEM((1, npass), I32),
            pltpu.VMEM(pattern.shape, I32),
            pltpu.VMEM((docs, nq), F32),
            pltpu.VMEM((nq, dim), BF16),
            pltpu.VMEM((ndoc * CAP, dim), BF16),
            pltpu.VMEM((ndoc // 2, 2, 8, 128), jnp.int16),
            pltpu.VMEM((ndoc, 8, 128), jnp.int16),
            pltpu.VMEM((ndoc, 8, 128), F32),
            pltpu.VMEM((ndoc, 1, 128), F32),
            pltpu.VMEM((ndoc, 1, 128), F32),
            pltpu.VMEM((ndoc, 8, 128), I32),
            pltpu.VMEM((ndoc * 8, 128), BF16),
            pltpu.VMEM((128, ndoc * 8), BF16),
            pltpu.VMEM((2 * MAXP, 128), F32),
            pltpu.VMEM((2, 8, 128), F32),
            pltpu.VMEM((nqry, 8, 128), F32),
            pltpu.VMEM((1, 128), F32),
            pltpu.VMEM((ndoc, 1, 128), F32),
            dma((5,)), regular, regular, regular,
            dma((6,)), dma((6,)), dma((7,)), dma((7,)),
            dma, dma, dma, dma, dma, dma, dma, dma,
        ],
        compiler_params=pltpu.CompilerParams(
            collective_id=0, has_side_effects=True, vmem_limit_bytes=60 * 1024 * 1024
        ),
    )(queries, passages, route.reshape(1, npass), pattern, teacher.T)
    return pooled.T, divergence.reshape(rows_dev)


def solution(mesh):
    split = Mesh(mesh.devices.reshape(4, -1, 4, 2), AXES)
    ny, nz, nx = (split.shape[a] for a in ("y", "z", "x"))
    placed = (P(("x", "c"), None), P(AXES, None), P(AXES), P(), P(None, AXES))
    return jax.shard_map(
        functools.partial(on_device, ny, nz, nx),
        mesh=split,
        in_specs=placed,
        out_specs=(P(None, AXES), P(("x", "c"))),
        check_vma=False,
    )
```

```python
import functools
import math

import jax
import jax.numpy as jnp
from jax import lax
from jax.experimental import pallas as pl
from jax.experimental.pallas import tpu as pltpu
from jax.sharding import Mesh
from jax.sharding import PartitionSpec as P

MESH = pl.DeviceIdType.MESH
AXES = ("y", "z", "x", "c")
F32, BF16, I32 = jnp.float32, jnp.bfloat16, jnp.int32
SCALE = 0.03125
LOW = -1e30
LIMIT = 14.0
TOP_CODE = 32767.0
CAP = 4
MAXP = 16


def mod(a, n):
    return lax.rem(a + 2 * n, n)


def kernel(
    ny, nz, nx,
    q_ref, p_hbm, route_hbm, pat_hbm, teach_hbm,
    docs_ref, div_ref,
    p_ref, route_ref, pat_ref, teach_ref, q1, q2, pperm, send1, send2, recv1, recv2, value, id_send, id_recv, doc_of, onehot, onehot_t, top,
    stat, stat_got, row, row_got,
    in_sem, z2_sem, z4_sem, y_sem, qs_sem, qr_sem, cs_sem, cr_sem, ids_sem, idr_sem, ss_sem, sr_sem,
    xs_sem, xr_sem, ds_sem, dr_sem,
):
    y, z = lax.axis_index("y"), lax.axis_index("z")
    x, c = lax.axis_index("x"), lax.axis_index("c")
    ndoc, nqry = ny * nz, nx * 2
    me_doc, me_qry = y * nz + z, x * 2 + c
    right, left = mod(x + 1, nx), mod(x - 1, nx)
    npass = p_hbm.shape[0]
    slots = ndoc * CAP

    barrier = pltpu.get_barrier_semaphore()

    along_y = [mod(y + k, ny) for k in range(ny)]

    def each_doc_peer(body):
        def step(k, carry):
            half = lax.div(k + 1, 2)
            pz = mod(z + nz // 2 + jnp.where(lax.rem(k, 2) == 0, half, -half), nz)
            for py in along_y:
                body(py, pz)
            return carry

        lax.fori_loop(0, nz - 1, step, 0)
        for py in along_y[1:]:
            body(py, z)

    def each_qry_peer(body):
        for k in range(1, nqry):
            peer = mod(me_qry + k, nqry)
            body(peer, lax.div(peer, 2), lax.rem(peer, 2))

    half = q_ref.shape[0] // 2
    own_rows = pl.ds(pl.multiple_of(c * (2 * half), 2 * half), 2 * half)
    loads = [
        pltpu.make_async_copy(src, dst, in_sem.at[k])
        for k, (src, dst) in enumerate((
            (route_hbm, route_ref), (p_hbm, p_ref), (teach_hbm, teach_ref), (pat_hbm, pat_ref),
            (q_ref, q1.at[own_rows]),
        ))
    ]
    for load in loads:
        load.start()

    def tell(sem, **to):
        pl.semaphore_signal(sem, inc=1, device_id=to, device_id_type=MESH)

    tell(barrier, x=right)
    tell(barrier, x=left)
    tell(barrier, c=1 - c)
    for k in (1, -1, 2, -2):
        tell(barrier, z=mod(z + k, nz))
    for k in range(1, ny):
        tell(barrier, y=mod(y + k, ny))
    pl.semaphore_wait(barrier, 7 + ny - 1)


    side = 4 * half
    places = ((q1, side), (q2, side + half), (q2, 0), (q1, side + half), (q2, side), (q2, half))

    def piece(k, core):
        part, at = places[k]
        return part.at[pl.ds(pl.multiple_of(at + core * (2 * half), half), half)]

    def x_copy(src, k, to_x):
        return pltpu.make_async_remote_copy(
            src_ref=src, dst_ref=piece(k, c), send_sem=qs_sem.at[k], recv_sem=qr_sem.at[k],
            device_id={"x": to_x}, device_id_type=MESH,
        )

    def c_copy(src, dst, k):
        return pltpu.make_async_remote_copy(
            src_ref=src, dst_ref=dst, send_sem=cs_sem.at[k], recv_sem=cr_sem.at[k],
            device_id={"c": 1 - c}, device_id_type=MESH,
        )

    sends = [
        x_copy(q_ref.at[pl.ds(0, half)], 0, right),
        x_copy(q_ref.at[pl.ds(half, half)], 3, left),
        c_copy(q_ref, q1.at[own_rows], 0),
        x_copy(q_ref.at[pl.ds(half, half)], 1, right),
        x_copy(q_ref.at[pl.ds(0, half)], 4, left),
    ]
    for s in sends:
        s.start()

    def tell_z(sem, far):
        tell(sem, z=mod(z + far, nz))
        tell(sem, z=mod(z - far, nz))

    def collect(*pieces):
        for k in pieces:
            got = piece(k, c)
            x_copy(got, k, right).wait_recv()
            if k == 0:
                sends.append(x_copy(got, 2, right))
                sends[-1].start()
            if k == 3:
                sends.append(x_copy(got, 5, left))
                sends[-1].start()
            sends.append(c_copy(got, got, k + 1))
            sends[-1].start()

    def from_partner(*pieces):
        for k in pieces:
            there = piece(k, 1 - c)
            c_copy(there, there, k + 1).wait_recv()

    tell_z(z2_sem, 2)

    loads[0].wait()
    route = route_ref[...]
    target = lax.shift_right_logical(route, 8 + (nqry.bit_length() - 1))
    to = lax.broadcasted_iota(I32, (ndoc, npass), 0) == target
    tri = (
        lax.broadcasted_iota(I32, (npass, npass), 0) < lax.broadcasted_iota(I32, (npass, npass), 1)
    ).astype(F32).astype(BF16)
    ahead = jnp.dot(to.astype(F32).astype(BF16), tri, preferred_element_type=F32)
    rank = jnp.sum(jnp.where(to, ahead, 0.0), axis=0, keepdims=True).astype(I32)
    place = target * CAP + rank
    put = lax.broadcasted_iota(I32, (slots, npass), 0) == place
    put_b = put.astype(F32).astype(BF16)
    local = jnp.bitwise_and(route, 255) // MAXP + 1

    width = 512

    def permute(k, carry):
        cols = pl.ds(pl.multiple_of(k * width, width), width)
        pperm[:, cols] = jnp.dot(put_b, p_ref[:, cols], preferred_element_type=F32).astype(BF16)
        return carry

    loads[1].wait()
    chunks = p_ref.shape[1] // width
    pl.semaphore_wait(z2_sem, 2)
    tell_z(z4_sem, 4)
    lax.fori_loop(0, chunks // 2, permute, 0)
    pl.semaphore_wait(z4_sem, 2)
    for k in range(1, ny):
        tell(y_sem, y=mod(y + k, ny))
    lax.fori_loop(chunks // 2, chunks, permute, 0)
    owner_rows = lax.broadcasted_iota(I32, (ndoc, npass), 0)
    lane = lax.broadcasted_iota(I32, (ndoc, 128), 1)
    ids = jnp.zeros((ndoc, 128), F32)
    for j in range(CAP):
        hit = jnp.where(owner_rows * CAP + j == place, local.astype(F32), 0.0)
        ids = jnp.where(lax.rem(lane, CAP) == j, jnp.sum(hit, axis=1, keepdims=True), ids)
    id_send[...] = ids.reshape(ndoc, 1, 128)
    collect(0, 3)
    pl.semaphore_wait(y_sem, ny - 1)

    steps = TOP_CODE / math.log(1.0 + 2.0 * LIMIT * LIMIT * SCALE * q_ref.shape[1])

    def exchange(part, send, recv, send_sem, recv_sem):
        scores = lax.dot_general(
            pperm[...], part[...], (((1,), (1,)), ((), ())), preferred_element_type=F32
        ) * SCALE
        size = jnp.floor(jnp.log(1.0 + 2.0 * jnp.abs(scores)) * steps + 0.5)
        codes = jnp.where(scores < 0.0, -size, size).astype(I32)
        send[...] = codes.reshape(ndoc, CAP, 128).astype(jnp.int16)

        def send_scores(py, pz):
            pltpu.make_async_remote_copy(
                src_ref=send.at[py * nz + pz], dst_ref=recv.at[me_doc], send_sem=send_sem, recv_sem=recv_sem,
                device_id={"y": py, "z": pz}, device_id_type=MESH,
            ).start()

        each_doc_peer(send_scores)
        recv[me_doc] = send[me_doc]

    loads[4].wait()
    c_copy(q_ref, q1.at[own_rows], 0).wait_recv()
    from_partner(0, 3)
    exchange(q1, send1, recv1, ss_sem.at[0], sr_sem.at[0])

    def send_id(py, pz):
        pltpu.make_async_remote_copy(
            src_ref=id_send.at[py * nz + pz], dst_ref=id_recv.at[me_doc], send_sem=ids_sem, recv_sem=idr_sem,
            device_id={"y": py, "z": pz}, device_id_type=MESH,
        ).start()

    each_doc_peer(send_id)
    id_recv[me_doc] = id_send[me_doc]

    collect(1, 4)

    loads[2].wait()
    loads[3].wait()
    teach = teach_ref[...]
    t_top = jnp.max(teach, axis=0, keepdims=True)
    t_exp = jnp.exp(teach - t_top)
    t_sum = jnp.sum(t_exp, axis=0, keepdims=True)
    t_weight = t_exp / t_sum
    t_total = t_top + jnp.log(t_sum)
    group = me_doc * nqry + me_qry
    col = jnp.sum(
        jnp.where(lax.broadcasted_iota(I32, pat_ref.shape, 1) == group, pat_ref[...], 0).astype(F32),
        axis=1, keepdims=True,
    )
    nq = teach.shape[1]
    per = nq // nqry
    spread = lax.broadcasted_iota(I32, (nqry, nq), 1) // per == lax.broadcasted_iota(I32, (nqry, nq), 0)
    active = jnp.sum(jnp.where(spread, col, 0.0), axis=0, keepdims=True) > 0.5

    collect(2, 5)
    from_partner(1, 4, 2, 5)
    exchange(q2, send2, recv2, ss_sem.at[1], sr_sem.at[1])

    pltpu.make_async_copy(id_recv.at[pl.ds(0, ndoc - 1)], id_recv.at[pl.ds(0, ndoc - 1)], idr_sem).wait()
    pltpu.make_async_copy(id_send.at[pl.ds(0, ndoc - 1)], id_send.at[pl.ds(0, ndoc - 1)], ids_sem).wait()
    got = id_recv[...].reshape(ndoc, 128).astype(BF16)
    wide = (
        lax.broadcasted_iota(I32, (slots, ndoc), 0) // CAP == lax.broadcasted_iota(I32, (slots, ndoc), 1)
    ).astype(F32).astype(BF16)
    lines = jnp.dot(wide, got, preferred_element_type=F32)
    r_i = lax.broadcasted_iota(I32, (slots, 128), 0)
    l_i = lax.broadcasted_iota(I32, (slots, 128), 1)
    mine = jnp.sum(jnp.where(lax.rem(r_i, CAP) == l_i, lines, 0.0), axis=1, keepdims=True)
    doc = jnp.broadcast_to(mine, (slots, 128)).astype(I32) - 1
    doc_of[...] = doc.reshape(slots // 8, 8, 128)
    hot = (doc == l_i).astype(F32)
    onehot[...] = hot.astype(BF16)
    onehot_t[...] = hot.T.astype(BF16)

    def all_blocks(ref, sem):
        return pltpu.make_async_copy(ref.at[pl.ds(0, ndoc - 1)], ref.at[pl.ds(0, ndoc - 1)], sem)

    def pool(recv):
        def tops(v, best):
            got = jnp.concatenate(
                [recv[2 * v].astype(I32).astype(F32), recv[2 * v + 1].astype(I32).astype(F32)], axis=0
            )
            size = 0.5 * (jnp.exp(jnp.abs(got) / steps) - 1.0)
            val, d = jnp.where(got < 0.0, -size, size), doc_of[v]
            value[v] = val
            return tuple(jnp.maximum(b, jnp.where(d == t, val, LOW)) for t, b in enumerate(best))

        best = lax.fori_loop(
            0, slots // 8, tops, tuple(jnp.full((8, 128), LOW, F32) for _ in range(MAXP)), unroll=4
        )
        for t in range(MAXP):
            top[t : t + 1] = jnp.max(best[t], axis=0, keepdims=True)
        top_b = top[...].astype(BF16)
        pad = jnp.zeros((128 - MAXP, 128), BF16)
        of_row = jnp.dot(onehot[...], jnp.concatenate([top_b, pad], axis=0), preferred_element_type=F32)
        e = jnp.exp(value[...].reshape(slots, 128) - of_row)
        e_hi = e.astype(BF16)
        e_lo = (e - e_hi.astype(F32)).astype(BF16)
        total = jnp.dot(onehot_t[...], e_hi, preferred_element_type=F32) + jnp.dot(
            onehot_t[...], e_lo, preferred_element_type=F32
        )
        return top_b.astype(F32) + jnp.log(total[:MAXP])

    all_blocks(recv1, sr_sem.at[0]).wait()
    pool1 = pool(recv1)
    all_blocks(recv2, sr_sem.at[1]).wait()
    pool2 = pool(recv2)
    lane_p = lax.broadcasted_iota(I32, pool1.shape, 1)
    back_half = lax.rem(lane_p, 2 * half) >= half
    near = jnp.where((lane_p < side) | back_half, pool1, pool2)
    away = jnp.where((lane_p < side) | back_half, pool2, pool1)
    pooled = pltpu.roll(jnp.concatenate([near, away], axis=1), x * side, 1)
    docs_ref[...] = jnp.where(active, pooled, 0.0)

    s_top = jnp.max(pooled, axis=0, keepdims=True)
    s_total = s_top + jnp.log(jnp.sum(jnp.exp(pooled - s_top), axis=0, keepdims=True))
    mean = jnp.sum(t_weight * (teach - pooled), axis=0, keepdims=True)
    s_total = jnp.where(active, s_total, LOW)
    t_tot = jnp.where(active, t_total, LOW)
    mean = jnp.where(active, mean, 0.0)
    fill = jnp.zeros((5, nq), F32)
    stats = jnp.concatenate([s_total, t_tot, mean, fill], axis=0)
    stat[0] = stats[:, :128]
    stat[1] = stats[:, 128:]

    def send_stat(peer, px, pc):
        pltpu.make_async_remote_copy(
            src_ref=stat.at[lax.div(peer * per, 128)], dst_ref=stat_got.at[me_qry], send_sem=xs_sem,
            recv_sem=xr_sem, device_id={"x": px, "c": pc}, device_id_type=MESH,
        ).start()

    each_qry_peer(send_stat)
    stat_got[me_qry] = stat[lax.div(me_qry * per, 128)]
    pltpu.make_async_copy(stat_got.at[pl.ds(0, nqry - 1)], stat_got.at[pl.ds(0, nqry - 1)], xr_sem).wait()
    part = stat_got[...]
    peak = jnp.max(part, axis=0)
    mass = jnp.exp(part - peak[None])
    summed = jnp.sum(mass, axis=0)
    totals = peak + jnp.log(summed)
    mean8 = jnp.sum(mass[:, 1:2] * part[:, 2:3], axis=0) / summed[1:2]
    shift = lax.rem(me_qry * per, 128)
    turn = mod(-shift, 128)
    lane1 = lax.broadcasted_iota(I32, (1, 128), 1)
    r0 = pltpu.roll(totals[0:1], turn, 1)
    r1 = pltpu.roll(totals[1:2], lax.rem(turn + per, 128), 1)
    r2 = pltpu.roll(mean8, lax.rem(turn + 2 * per, 128), 1)
    line = jnp.where(lane1 < per, r0, jnp.where(lane1 < 2 * per, r1, r2))
    row[...] = line
    row_got[me_doc] = line

    def send_row(py, pz):
        pltpu.make_async_remote_copy(
            src_ref=row, dst_ref=row_got.at[me_doc], send_sem=ds_sem, recv_sem=dr_sem,
            device_id={"y": py, "z": pz}, device_id_type=MESH,
        ).start()

    each_doc_peer(send_row)
    pltpu.make_async_copy(row_got.at[pl.ds(0, ndoc - 1)], row_got.at[pl.ds(0, ndoc - 1)], dr_sem).wait()
    rows = row_got[...].reshape(ndoc, 128)
    peak = jnp.max(rows, axis=0, keepdims=True)
    mass = jnp.exp(rows - peak)
    summed = jnp.sum(mass, axis=0, keepdims=True)
    totals = peak + jnp.log(summed)
    weighted = jnp.sum(pltpu.roll(mass, per, 1) * rows, axis=0, keepdims=True)
    at2 = weighted / pltpu.roll(summed, per, 1)
    out = pltpu.roll(at2, 128 - 2 * per, 1) - pltpu.roll(totals, 128 - per, 1) + totals
    div_ref[...] = out[:, :per]

    all_blocks(recv1, ss_sem.at[0]).wait()
    all_blocks(recv2, ss_sem.at[1]).wait()
    for t in sends:
        t.wait_send()
    pltpu.make_async_copy(stat_got.at[pl.ds(0, nqry - 1)], stat_got.at[pl.ds(0, nqry - 1)], xs_sem).wait()
    pltpu.make_async_copy(row_got.at[pl.ds(0, ndoc - 1)], row_got.at[pl.ds(0, ndoc - 1)], ds_sem).wait()


def on_device(ny, nz, nx, queries, passages, route, pattern, teacher):
    ndoc, nqry = ny * nz, nx * 2
    npass, dim = passages.shape
    rows_dev = queries.shape[0]
    nq, docs = teacher.shape
    vmem = pl.BlockSpec(memory_space=pltpu.VMEM)
    hbm = pl.BlockSpec(memory_space=pltpu.HBM)
    dma, regular = pltpu.SemaphoreType.DMA, pltpu.SemaphoreType.REGULAR
    inputs = (queries, passages, route.reshape(1, npass), pattern, teacher.T)
    pooled, divergence = pl.pallas_call(
        functools.partial(kernel, ny, nz, nx),
        out_shape=(
            jax.ShapeDtypeStruct((docs, nq), F32),
            jax.ShapeDtypeStruct((1, rows_dev), F32),
        ),
        in_specs=[hbm] * 5,
        out_specs=(vmem, vmem),
        scratch_shapes=[
            pltpu.VMEM((npass, dim), BF16),
            pltpu.VMEM((1, npass), I32),
            pltpu.VMEM(pattern.shape, I32),
            pltpu.VMEM((docs, nq), F32),
            pltpu.VMEM((nq // 2, dim), BF16),
            pltpu.VMEM((nq // 2, dim), BF16),
            pltpu.VMEM((ndoc * CAP, dim), BF16),
            pltpu.VMEM((ndoc, CAP, 128), jnp.int16),
            pltpu.VMEM((ndoc, CAP, 128), jnp.int16),
            pltpu.VMEM((ndoc, CAP, 128), jnp.int16),
            pltpu.VMEM((ndoc, CAP, 128), jnp.int16),
            pltpu.VMEM((ndoc * CAP // 8, 8, 128), F32),
            pltpu.VMEM((ndoc, 1, 128), F32),
            pltpu.VMEM((ndoc, 1, 128), F32),
            pltpu.VMEM((ndoc * CAP // 8, 8, 128), I32),
            pltpu.VMEM((ndoc * CAP, 128), BF16),
            pltpu.VMEM((128, ndoc * CAP), BF16),
            pltpu.VMEM((MAXP, 128), F32),
            pltpu.VMEM((2, 8, 128), F32),
            pltpu.VMEM((nqry, 8, 128), F32),
            pltpu.VMEM((1, 128), F32),
            pltpu.VMEM((ndoc, 1, 128), F32),
            dma((5,)), regular, regular, regular,
            dma((6,)), dma((6,)), dma((7,)), dma((7,)),
            dma, dma, dma((2,)), dma((2,)), dma, dma, dma, dma,
        ],
        compiler_params=pltpu.CompilerParams(
            collective_id=0, has_side_effects=True, vmem_limit_bytes=32 * 1024 * 1024
        ),
    )(*(pltpu.with_memory_space_constraint(a, pltpu.HBM) for a in inputs))
    return pooled.T, divergence.reshape(rows_dev)


def solution(mesh):
    split = Mesh(mesh.devices.reshape(4, -1, 4, 2), AXES)
    ny, nz, nx = (split.shape[a] for a in ("y", "z", "x"))
    placed = (P(("x", "c"), None), P(AXES, None), P(AXES), P(), P(None, AXES))
    return jax.shard_map(
        functools.partial(on_device, ny, nz, nx),
        mesh=split,
        in_specs=placed,
        out_specs=(P(None, AXES), P(("x", "c"))),
        check_vma=False,
    )
```

```python
import functools
import math

import jax
import jax.numpy as jnp
from jax import lax
from jax.experimental import pallas as pl
from jax.experimental.pallas import tpu as pltpu
from jax.sharding import Mesh
from jax.sharding import PartitionSpec as P

MESH = pl.DeviceIdType.MESH
AXES = ("y", "z", "x", "c")
F32, BF16, I32 = jnp.float32, jnp.bfloat16, jnp.int32
SCALE = 0.03125
LOW = -1e30
LIMIT = 14.0
TOP_CODE = 32767.0
CAP = 4
MAXP = 16


def mod(a, n):
    return lax.rem(a + 2 * n, n)


def kernel(
    ny, nz, nx,
    q_ref, p_hbm, route_hbm, pat_hbm, teach_hbm,
    docs_ref, div_ref,
    p_ref, route_ref, pat_ref, teach_ref, q1, q2, pperm, send1, send2, recv1, recv2, value, id_send, id_recv, doc_of, onehot, onehot_t, top,
    stat, stat_got, row, row_got,
    in_sem, z2_sem, z4_sem, y_sem, qs_sem, qr_sem, cs_sem, cr_sem, ids_sem, idr_sem, ss_sem, sr_sem,
    xs_sem, xr_sem, ds_sem, dr_sem,
):
    y, z = lax.axis_index("y"), lax.axis_index("z")
    x, c = lax.axis_index("x"), lax.axis_index("c")
    ndoc, nqry = ny * nz, nx * 2
    me_doc, me_qry = y * nz + z, x * 2 + c
    right, left = mod(x + 1, nx), mod(x - 1, nx)
    npass = p_hbm.shape[0]
    slots = ndoc * CAP

    barrier = pltpu.get_barrier_semaphore()

    along_y = [mod(y + k, ny) for k in range(ny)]

    def each_doc_peer(body):
        def step(k, carry):
            half = lax.div(k + 1, 2)
            pz = mod(z + nz // 2 + jnp.where(lax.rem(k, 2) == 0, half, -half), nz)
            for py in along_y:
                body(py, pz)
            return carry

        lax.fori_loop(0, nz - 1, step, 0)
        for py in along_y[1:]:
            body(py, z)

    def each_qry_peer(body):
        for k in range(1, nqry):
            peer = mod(me_qry + k, nqry)
            body(peer, lax.div(peer, 2), lax.rem(peer, 2))

    half = q_ref.shape[0] // 2
    own_rows = pl.ds(pl.multiple_of(c * (2 * half), 2 * half), 2 * half)
    loads = [
        pltpu.make_async_copy(src, dst, in_sem.at[k])
        for k, (src, dst) in enumerate((
            (q_ref, q1.at[own_rows]), (route_hbm, route_ref), (p_hbm, p_ref), (teach_hbm, teach_ref),
            (pat_hbm, pat_ref),
        ))
    ]
    for load in loads:
        load.start()

    def tell(sem, **to):
        pl.semaphore_signal(sem, inc=1, device_id=to, device_id_type=MESH)

    tell(barrier, x=right)
    tell(barrier, x=left)
    tell(barrier, c=1 - c)
    for k in (1, -1, 2, -2):
        tell(barrier, z=mod(z + k, nz))
    for k in range(1, ny):
        tell(barrier, y=mod(y + k, ny))
    pl.semaphore_wait(barrier, 7 + ny - 1)


    side = 4 * half
    places = ((q1, side), (q2, side + half), (q2, 0), (q1, side + half), (q2, side), (q2, half))

    def piece(k, core):
        part, at = places[k]
        return part.at[pl.ds(pl.multiple_of(at + core * (2 * half), half), half)]

    def x_copy(src, k, to_x):
        return pltpu.make_async_remote_copy(
            src_ref=src, dst_ref=piece(k, c), send_sem=qs_sem.at[k], recv_sem=qr_sem.at[k],
            device_id={"x": to_x}, device_id_type=MESH,
        )

    def c_copy(src, dst, k):
        return pltpu.make_async_remote_copy(
            src_ref=src, dst_ref=dst, send_sem=cs_sem.at[k], recv_sem=cr_sem.at[k],
            device_id={"c": 1 - c}, device_id_type=MESH,
        )

    loads[0].wait()
    own = [q1.at[pl.ds(pl.multiple_of(c * (2 * half) + h * half, half), half)] for h in (0, 1)]
    sends = [
        x_copy(own[0], 0, right),
        x_copy(own[1], 3, left),
        c_copy(q1.at[own_rows], q1.at[own_rows], 0),
        x_copy(own[1], 1, right),
        x_copy(own[0], 4, left),
    ]
    for s in sends:
        s.start()

    def tell_z(sem, far):
        tell(sem, z=mod(z + far, nz))
        tell(sem, z=mod(z - far, nz))

    def collect(*pieces):
        for k in pieces:
            got = piece(k, c)
            x_copy(got, k, right).wait_recv()
            if k == 0:
                sends.append(x_copy(got, 2, right))
                sends[-1].start()
            if k == 3:
                sends.append(x_copy(got, 5, left))
                sends[-1].start()
            sends.append(c_copy(got, got, k + 1))
            sends[-1].start()

    def from_partner(*pieces):
        for k in pieces:
            there = piece(k, 1 - c)
            c_copy(there, there, k + 1).wait_recv()

    tell_z(z2_sem, 2)

    loads[1].wait()
    route = route_ref[...]
    target = lax.shift_right_logical(route, 8 + (nqry.bit_length() - 1))
    to = lax.broadcasted_iota(I32, (ndoc, npass), 0) == target
    tri = (
        lax.broadcasted_iota(I32, (npass, npass), 0) < lax.broadcasted_iota(I32, (npass, npass), 1)
    ).astype(F32).astype(BF16)
    ahead = jnp.dot(to.astype(F32).astype(BF16), tri, preferred_element_type=F32)
    rank = jnp.sum(jnp.where(to, ahead, 0.0), axis=0, keepdims=True).astype(I32)
    place = target * CAP + rank
    put = lax.broadcasted_iota(I32, (slots, npass), 0) == place
    put_b = put.astype(F32).astype(BF16)
    local = jnp.bitwise_and(route, 255) // MAXP + 1

    width = 512

    def permute(k, carry):
        cols = pl.ds(pl.multiple_of(k * width, width), width)
        pperm[:, cols] = jnp.dot(put_b, p_ref[:, cols], preferred_element_type=F32).astype(BF16)
        return carry

    loads[2].wait()
    chunks = p_ref.shape[1] // width
    pl.semaphore_wait(z2_sem, 2)
    tell_z(z4_sem, 4)
    lax.fori_loop(0, chunks, permute, 0)

    owner_rows = lax.broadcasted_iota(I32, (ndoc, npass), 0)
    lane = lax.broadcasted_iota(I32, (ndoc, 128), 1)
    ids = jnp.zeros((ndoc, 128), F32)
    for j in range(CAP):
        hit = jnp.where(owner_rows * CAP + j == place, local.astype(F32), 0.0)
        ids = jnp.where(lax.rem(lane, CAP) == j, jnp.sum(hit, axis=1, keepdims=True), ids)
    id_send[...] = ids.reshape(ndoc, 1, 128)
    collect(0, 3)
    pl.semaphore_wait(z4_sem, 2)
    for k in range(1, ny):
        tell(y_sem, y=mod(y + k, ny))
    pl.semaphore_wait(y_sem, ny - 1)

    steps = TOP_CODE / math.log(1.0 + 2.0 * LIMIT * LIMIT * SCALE * q_ref.shape[1])

    def exchange(part, send, recv, send_sem, recv_sem):
        scores = lax.dot_general(
            pperm[...], part[...], (((1,), (1,)), ((), ())), preferred_element_type=F32
        ) * SCALE
        size = jnp.floor(jnp.log(1.0 + 2.0 * jnp.abs(scores)) * steps + 0.5)
        codes = jnp.where(scores < 0.0, -size, size).astype(I32)
        send[...] = codes.reshape(ndoc, CAP, 128).astype(jnp.int16)

        def send_scores(py, pz):
            pltpu.make_async_remote_copy(
                src_ref=send.at[py * nz + pz], dst_ref=recv.at[me_doc], send_sem=send_sem, recv_sem=recv_sem,
                device_id={"y": py, "z": pz}, device_id_type=MESH,
            ).start()

        each_doc_peer(send_scores)
        recv[me_doc] = send[me_doc]

    c_copy(q1.at[own_rows], q1.at[own_rows], 0).wait_recv()
    from_partner(0, 3)
    exchange(q1, send1, recv1, ss_sem.at[0], sr_sem.at[0])

    def send_id(py, pz):
        pltpu.make_async_remote_copy(
            src_ref=id_send.at[py * nz + pz], dst_ref=id_recv.at[me_doc], send_sem=ids_sem, recv_sem=idr_sem,
            device_id={"y": py, "z": pz}, device_id_type=MESH,
        ).start()

    each_doc_peer(send_id)
    id_recv[me_doc] = id_send[me_doc]

    collect(1, 4)

    loads[3].wait()
    loads[4].wait()
    teach = teach_ref[...]
    t_top = jnp.max(teach, axis=0, keepdims=True)
    t_exp = jnp.exp(teach - t_top)
    t_sum = jnp.sum(t_exp, axis=0, keepdims=True)
    t_weight = t_exp / t_sum
    t_total = t_top + jnp.log(t_sum)
    group = me_doc * nqry + me_qry
    col = jnp.sum(
        jnp.where(lax.broadcasted_iota(I32, pat_ref.shape, 1) == group, pat_ref[...], 0).astype(F32),
        axis=1, keepdims=True,
    )
    nq = teach.shape[1]
    per = nq // nqry
    spread = lax.broadcasted_iota(I32, (nqry, nq), 1) // per == lax.broadcasted_iota(I32, (nqry, nq), 0)
    active = jnp.sum(jnp.where(spread, col, 0.0), axis=0, keepdims=True) > 0.5

    collect(2, 5)
    from_partner(1, 4, 2, 5)
    exchange(q2, send2, recv2, ss_sem.at[1], sr_sem.at[1])

    pltpu.make_async_copy(id_recv.at[pl.ds(0, ndoc - 1)], id_recv.at[pl.ds(0, ndoc - 1)], idr_sem).wait()
    pltpu.make_async_copy(id_send.at[pl.ds(0, ndoc - 1)], id_send.at[pl.ds(0, ndoc - 1)], ids_sem).wait()
    got = id_recv[...].reshape(ndoc, 128).astype(BF16)
    wide = (
        lax.broadcasted_iota(I32, (slots, ndoc), 0) // CAP == lax.broadcasted_iota(I32, (slots, ndoc), 1)
    ).astype(F32).astype(BF16)
    lines = jnp.dot(wide, got, preferred_element_type=F32)
    r_i = lax.broadcasted_iota(I32, (slots, 128), 0)
    l_i = lax.broadcasted_iota(I32, (slots, 128), 1)
    mine = jnp.sum(jnp.where(lax.rem(r_i, CAP) == l_i, lines, 0.0), axis=1, keepdims=True)
    doc = jnp.broadcast_to(mine, (slots, 128)).astype(I32) - 1
    doc_of[...] = doc.reshape(slots // 8, 8, 128)
    hot = (doc == l_i).astype(F32)
    onehot[...] = hot.astype(BF16)
    onehot_t[...] = hot.T.astype(BF16)

    def all_blocks(ref, sem):
        return pltpu.make_async_copy(ref.at[pl.ds(0, ndoc - 1)], ref.at[pl.ds(0, ndoc - 1)], sem)

    def pool(recv):
        def tops(v, best):
            got = jnp.concatenate(
                [recv[2 * v].astype(I32).astype(F32), recv[2 * v + 1].astype(I32).astype(F32)], axis=0
            )
            size = 0.5 * (jnp.exp(jnp.abs(got) / steps) - 1.0)
            val, d = jnp.where(got < 0.0, -size, size), doc_of[v]
            value[v] = val
            return tuple(jnp.maximum(b, jnp.where(d == t, val, LOW)) for t, b in enumerate(best))

        best = lax.fori_loop(
            0, slots // 8, tops, tuple(jnp.full((8, 128), LOW, F32) for _ in range(MAXP)), unroll=4
        )
        for t in range(MAXP):
            top[t : t + 1] = jnp.max(best[t], axis=0, keepdims=True)
        top_b = top[...].astype(BF16)
        pad = jnp.zeros((128 - MAXP, 128), BF16)
        of_row = jnp.dot(onehot[...], jnp.concatenate([top_b, pad], axis=0), preferred_element_type=F32)
        e = jnp.exp(value[...].reshape(slots, 128) - of_row)
        e_hi = e.astype(BF16)
        e_lo = (e - e_hi.astype(F32)).astype(BF16)
        total = jnp.dot(onehot_t[...], e_hi, preferred_element_type=F32) + jnp.dot(
            onehot_t[...], e_lo, preferred_element_type=F32
        )
        return top_b.astype(F32) + jnp.log(total[:MAXP])

    all_blocks(recv1, sr_sem.at[0]).wait()
    pool1 = pool(recv1)
    all_blocks(recv2, sr_sem.at[1]).wait()
    pool2 = pool(recv2)
    lane_p = lax.broadcasted_iota(I32, pool1.shape, 1)
    back_half = lax.rem(lane_p, 2 * half) >= half
    near = jnp.where((lane_p < side) | back_half, pool1, pool2)
    away = jnp.where((lane_p < side) | back_half, pool2, pool1)
    pooled = pltpu.roll(jnp.concatenate([near, away], axis=1), x * side, 1)
    docs_ref[...] = jnp.where(active, pooled, 0.0)

    s_top = jnp.max(pooled, axis=0, keepdims=True)
    s_total = s_top + jnp.log(jnp.sum(jnp.exp(pooled - s_top), axis=0, keepdims=True))
    mean = jnp.sum(t_weight * (teach - pooled), axis=0, keepdims=True)
    s_total = jnp.where(active, s_total, LOW)
    t_tot = jnp.where(active, t_total, LOW)
    mean = jnp.where(active, mean, 0.0)
    fill = jnp.zeros((5, nq), F32)
    stats = jnp.concatenate([s_total, t_tot, mean, fill], axis=0)
    stat[0] = stats[:, :128]
    stat[1] = stats[:, 128:]

    def send_stat(peer, px, pc):
        pltpu.make_async_remote_copy(
            src_ref=stat.at[lax.div(peer * per, 128)], dst_ref=stat_got.at[me_qry], send_sem=xs_sem,
            recv_sem=xr_sem, device_id={"x": px, "c": pc}, device_id_type=MESH,
        ).start()

    each_qry_peer(send_stat)
    stat_got[me_qry] = stat[lax.div(me_qry * per, 128)]
    pltpu.make_async_copy(stat_got.at[pl.ds(0, nqry - 1)], stat_got.at[pl.ds(0, nqry - 1)], xr_sem).wait()
    part = stat_got[...]
    peak = jnp.max(part, axis=0)
    mass = jnp.exp(part - peak[None])
    summed = jnp.sum(mass, axis=0)
    totals = peak + jnp.log(summed)
    mean8 = jnp.sum(mass[:, 1:2] * part[:, 2:3], axis=0) / summed[1:2]
    shift = lax.rem(me_qry * per, 128)
    turn = mod(-shift, 128)
    lane1 = lax.broadcasted_iota(I32, (1, 128), 1)
    r0 = pltpu.roll(totals[0:1], turn, 1)
    r1 = pltpu.roll(totals[1:2], lax.rem(turn + per, 128), 1)
    r2 = pltpu.roll(mean8, lax.rem(turn + 2 * per, 128), 1)
    line = jnp.where(lane1 < per, r0, jnp.where(lane1 < 2 * per, r1, r2))
    row[...] = line
    row_got[me_doc] = line

    def send_row(py, pz):
        pltpu.make_async_remote_copy(
            src_ref=row, dst_ref=row_got.at[me_doc], send_sem=ds_sem, recv_sem=dr_sem,
            device_id={"y": py, "z": pz}, device_id_type=MESH,
        ).start()

    each_doc_peer(send_row)
    pltpu.make_async_copy(row_got.at[pl.ds(0, ndoc - 1)], row_got.at[pl.ds(0, ndoc - 1)], dr_sem).wait()
    rows = row_got[...].reshape(ndoc, 128)
    peak = jnp.max(rows, axis=0, keepdims=True)
    mass = jnp.exp(rows - peak)
    summed = jnp.sum(mass, axis=0, keepdims=True)
    totals = peak + jnp.log(summed)
    weighted = jnp.sum(pltpu.roll(mass, per, 1) * rows, axis=0, keepdims=True)
    at2 = weighted / pltpu.roll(summed, per, 1)
    out = pltpu.roll(at2, 128 - 2 * per, 1) - pltpu.roll(totals, 128 - per, 1) + totals
    div_ref[...] = out[:, :per]

    all_blocks(recv1, ss_sem.at[0]).wait()
    all_blocks(recv2, ss_sem.at[1]).wait()
    for t in sends:
        t.wait_send()
    pltpu.make_async_copy(stat_got.at[pl.ds(0, nqry - 1)], stat_got.at[pl.ds(0, nqry - 1)], xs_sem).wait()
    pltpu.make_async_copy(row_got.at[pl.ds(0, ndoc - 1)], row_got.at[pl.ds(0, ndoc - 1)], ds_sem).wait()


def hand_on(docs_ref, div_ref, docs_out, div_out, sem):
    copies = [
        pltpu.make_async_copy(docs_ref, docs_out, sem.at[0]),
        pltpu.make_async_copy(div_ref, div_out, sem.at[1]),
    ]
    for copy in copies:
        copy.start()
    for copy in copies:
        copy.wait()


def on_device(ny, nz, nx, queries, passages, route, pattern, teacher):
    ndoc, nqry = ny * nz, nx * 2
    npass, dim = passages.shape
    rows_dev = queries.shape[0]
    nq, docs = teacher.shape
    vmem = pl.BlockSpec(memory_space=pltpu.VMEM)
    hbm = pl.BlockSpec(memory_space=pltpu.HBM)
    dma, regular = pltpu.SemaphoreType.DMA, pltpu.SemaphoreType.REGULAR
    inputs = (queries, passages, route.reshape(1, npass), pattern, teacher.T)
    pooled, divergence = pl.pallas_call(
        functools.partial(kernel, ny, nz, nx),
        out_shape=(
            jax.ShapeDtypeStruct((docs, nq), F32),
            jax.ShapeDtypeStruct((1, rows_dev), F32),
        ),
        in_specs=[hbm] * 5,
        out_specs=(vmem, vmem),
        scratch_shapes=[
            pltpu.VMEM((npass, dim), BF16),
            pltpu.VMEM((1, npass), I32),
            pltpu.VMEM(pattern.shape, I32),
            pltpu.VMEM((docs, nq), F32),
            pltpu.VMEM((nq // 2, dim), BF16),
            pltpu.VMEM((nq // 2, dim), BF16),
            pltpu.VMEM((ndoc * CAP, dim), BF16),
            pltpu.VMEM((ndoc, CAP, 128), jnp.int16),
            pltpu.VMEM((ndoc, CAP, 128), jnp.int16),
            pltpu.VMEM((ndoc, CAP, 128), jnp.int16),
            pltpu.VMEM((ndoc, CAP, 128), jnp.int16),
            pltpu.VMEM((ndoc * CAP // 8, 8, 128), F32),
            pltpu.VMEM((ndoc, 1, 128), F32),
            pltpu.VMEM((ndoc, 1, 128), F32),
            pltpu.VMEM((ndoc * CAP // 8, 8, 128), I32),
            pltpu.VMEM((ndoc * CAP, 128), BF16),
            pltpu.VMEM((128, ndoc * CAP), BF16),
            pltpu.VMEM((MAXP, 128), F32),
            pltpu.VMEM((2, 8, 128), F32),
            pltpu.VMEM((nqry, 8, 128), F32),
            pltpu.VMEM((1, 128), F32),
            pltpu.VMEM((ndoc, 1, 128), F32),
            dma((5,)), regular, regular, regular,
            dma((6,)), dma((6,)), dma((7,)), dma((7,)),
            dma, dma, dma((2,)), dma((2,)), dma, dma, dma, dma,
        ],
        compiler_params=pltpu.CompilerParams(
            collective_id=0, has_side_effects=True, vmem_limit_bytes=32 * 1024 * 1024
        ),
    )(*(pltpu.with_memory_space_constraint(a, pltpu.HBM) for a in inputs))
    pooled, divergence = pl.pallas_call(
        hand_on,
        out_shape=(
            jax.ShapeDtypeStruct((docs, nq), F32),
            jax.ShapeDtypeStruct((1, rows_dev), F32),
        ),
        in_specs=[pl.BlockSpec(memory_space=pl.ANY)] * 2,
        out_specs=(hbm, hbm),
        scratch_shapes=[dma((2,))],
        compiler_params=pltpu.CompilerParams(vmem_limit_bytes=1024 * 1024),
    )(pooled, divergence)
    return pooled.T, divergence.reshape(rows_dev)


def solution(mesh):
    split = Mesh(mesh.devices.reshape(4, -1, 4, 2), AXES)
    ny, nz, nx = (split.shape[a] for a in ("y", "z", "x"))
    placed = (P(("x", "c"), None), P(AXES, None), P(AXES), P(), P(None, AXES))
    return jax.shard_map(
        functools.partial(on_device, ny, nz, nx),
        mesh=split,
        in_specs=placed,
        out_specs=(P(None, AXES), P(("x", "c"))),
        check_vma=False,
    )
```

```python
import functools
import math

import jax
import jax.numpy as jnp
from jax import lax
from jax.experimental import pallas as pl
from jax.experimental.pallas import tpu as pltpu
from jax.sharding import Mesh
from jax.sharding import PartitionSpec as P

MESH = pl.DeviceIdType.MESH
AXES = ("y", "z", "x", "c")
F32, BF16, I32 = jnp.float32, jnp.bfloat16, jnp.int32
SCALE = 0.03125
LOW = -1e30
LIMIT = 14.0
TOP_CODE = 32767.0
CAP = 4
MAXP = 16


def mod(a, n):
    return lax.rem(a + 2 * n, n)


def kernel(
    ny, nz, nx,
    q_ref, p_hbm, route_hbm, pat_hbm, teach_hbm,
    docs_ref, div_ref,
    p_ref, route_ref, pat_ref, teach_ref, q1, q2, pperm, send1, send2, recv1, recv2, value, id_send, id_recv, doc_of, onehot, onehot_t, top,
    stat, stat_got, row, row_got,
    in_sem, z2_sem, z4_sem, y_sem, qs_sem, qr_sem, cs_sem, cr_sem, ids_sem, idr_sem, ss_sem, sr_sem,
    xs_sem, xr_sem, ds_sem, dr_sem,
):
    y, z = lax.axis_index("y"), lax.axis_index("z")
    x, c = lax.axis_index("x"), lax.axis_index("c")
    ndoc, nqry = ny * nz, nx * 2
    me_doc, me_qry = y * nz + z, x * 2 + c
    right, left = mod(x + 1, nx), mod(x - 1, nx)
    npass = p_hbm.shape[0]
    slots = ndoc * CAP

    barrier = pltpu.get_barrier_semaphore()

    along_y = [mod(y + k, ny) for k in range(ny)]

    def each_doc_peer(body):
        def step(k, carry):
            half = lax.div(k + 1, 2)
            pz = mod(z + nz // 2 + jnp.where(lax.rem(k, 2) == 0, half, -half), nz)
            for py in along_y:
                body(py, pz)
            return carry

        lax.fori_loop(0, nz - 1, step, 0)
        for py in along_y[1:]:
            body(py, z)

    def each_qry_peer(body):
        for k in range(1, nqry):
            peer = mod(me_qry + k, nqry)
            body(peer, lax.div(peer, 2), lax.rem(peer, 2))

    half = q_ref.shape[0] // 2
    own_rows = pl.ds(pl.multiple_of(c * (2 * half), 2 * half), 2 * half)
    loads = [
        pltpu.make_async_copy(src, dst, in_sem.at[k])
        for k, (src, dst) in enumerate((
            (q_ref, q1.at[own_rows]), (route_hbm, route_ref), (p_hbm, p_ref), (teach_hbm, teach_ref),
            (pat_hbm, pat_ref),
        ))
    ]
    for load in loads:
        load.start()

    def tell(sem, **to):
        pl.semaphore_signal(sem, inc=1, device_id=to, device_id_type=MESH)

    tell(barrier, x=right)
    tell(barrier, x=left)
    tell(barrier, c=1 - c)
    for k in (1, -1, 2, -2):
        tell(barrier, z=mod(z + k, nz))
    for k in range(1, ny):
        tell(barrier, y=mod(y + k, ny))
    pl.semaphore_wait(barrier, 7 + ny - 1)


    side = 4 * half
    places = ((q1, side), (q2, side + half), (q2, 0), (q1, side + half), (q2, side), (q2, half))

    def piece(k, core):
        part, at = places[k]
        return part.at[pl.ds(pl.multiple_of(at + core * (2 * half), half), half)]

    def x_copy(src, k, to_x):
        return pltpu.make_async_remote_copy(
            src_ref=src, dst_ref=piece(k, c), send_sem=qs_sem.at[k], recv_sem=qr_sem.at[k],
            device_id={"x": to_x}, device_id_type=MESH,
        )

    def c_copy(src, dst, k):
        return pltpu.make_async_remote_copy(
            src_ref=src, dst_ref=dst, send_sem=cs_sem.at[k], recv_sem=cr_sem.at[k],
            device_id={"c": 1 - c}, device_id_type=MESH,
        )

    loads[0].wait()
    own = [q1.at[pl.ds(pl.multiple_of(c * (2 * half) + h * half, half), half)] for h in (0, 1)]
    sends = [
        x_copy(own[0], 0, right),
        x_copy(own[1], 3, left),
        c_copy(q1.at[own_rows], q1.at[own_rows], 0),
        x_copy(own[1], 1, right),
        x_copy(own[0], 4, left),
    ]
    for s in sends:
        s.start()

    def tell_z(sem, far):
        tell(sem, z=mod(z + far, nz))
        tell(sem, z=mod(z - far, nz))

    def collect(*pieces):
        for k in pieces:
            got = piece(k, c)
            x_copy(got, k, right).wait_recv()
            if k == 0:
                sends.append(x_copy(got, 2, right))
                sends[-1].start()
            if k == 3:
                sends.append(x_copy(got, 5, left))
                sends[-1].start()
            sends.append(c_copy(got, got, k + 1))
            sends[-1].start()

    def from_partner(*pieces):
        for k in pieces:
            there = piece(k, 1 - c)
            c_copy(there, there, k + 1).wait_recv()

    tell_z(z2_sem, 2)

    loads[1].wait()
    route = route_ref[...]
    target = lax.shift_right_logical(route, 8 + (nqry.bit_length() - 1))
    to = lax.broadcasted_iota(I32, (ndoc, npass), 0) == target
    tri = (
        lax.broadcasted_iota(I32, (npass, npass), 0) < lax.broadcasted_iota(I32, (npass, npass), 1)
    ).astype(F32).astype(BF16)
    ahead = jnp.dot(to.astype(F32).astype(BF16), tri, preferred_element_type=F32)
    rank = jnp.sum(jnp.where(to, ahead, 0.0), axis=0, keepdims=True).astype(I32)
    place = target * CAP + rank
    put = lax.broadcasted_iota(I32, (slots, npass), 0) == place
    put_b = put.astype(F32).astype(BF16)
    local = jnp.bitwise_and(route, 255) // MAXP + 1

    width = 512

    def permute(k, carry):
        cols = pl.ds(pl.multiple_of(k * width, width), width)
        pperm[:, cols] = jnp.dot(put_b, p_ref[:, cols], preferred_element_type=F32).astype(BF16)
        return carry

    loads[2].wait()
    chunks = p_ref.shape[1] // width
    pl.semaphore_wait(z2_sem, 2)
    tell_z(z4_sem, 4)
    lax.fori_loop(0, chunks, permute, 0)

    owner_rows = lax.broadcasted_iota(I32, (ndoc, npass), 0)
    lane = lax.broadcasted_iota(I32, (ndoc, 128), 1)
    ids = jnp.zeros((ndoc, 128), F32)
    for j in range(CAP):
        hit = jnp.where(owner_rows * CAP + j == place, local.astype(F32), 0.0)
        ids = jnp.where(lax.rem(lane, CAP) == j, jnp.sum(hit, axis=1, keepdims=True), ids)
    id_send[...] = ids.reshape(ndoc, 1, 128)
    collect(0, 3)
    pl.semaphore_wait(z4_sem, 2)
    for k in range(1, ny):
        tell(y_sem, y=mod(y + k, ny))
    pl.semaphore_wait(y_sem, ny - 1)

    steps = TOP_CODE / math.log(1.0 + 2.0 * LIMIT * LIMIT * SCALE * q_ref.shape[1])

    def exchange(part, send, recv, send_sem, recv_sem):
        scores = lax.dot_general(
            pperm[...], part[...], (((1,), (1,)), ((), ())), preferred_element_type=F32
        ) * SCALE
        size = jnp.floor(jnp.log(1.0 + 2.0 * jnp.abs(scores)) * steps + 0.5)
        codes = jnp.where(scores < 0.0, -size, size).astype(I32)
        send[...] = codes.reshape(ndoc, CAP, 128).astype(jnp.int16)

        def send_scores(py, pz):
            pltpu.make_async_remote_copy(
                src_ref=send.at[py * nz + pz], dst_ref=recv.at[me_doc], send_sem=send_sem, recv_sem=recv_sem,
                device_id={"y": py, "z": pz}, device_id_type=MESH,
            ).start()

        each_doc_peer(send_scores)
        recv[me_doc] = send[me_doc]

    c_copy(q1.at[own_rows], q1.at[own_rows], 0).wait_recv()
    from_partner(0, 3)
    exchange(q1, send1, recv1, ss_sem.at[0], sr_sem.at[0])
    collect(1, 4)

    def send_id(py, pz):
        pltpu.make_async_remote_copy(
            src_ref=id_send.at[py * nz + pz], dst_ref=id_recv.at[me_doc], send_sem=ids_sem, recv_sem=idr_sem,
            device_id={"y": py, "z": pz}, device_id_type=MESH,
        ).start()

    each_doc_peer(send_id)
    id_recv[me_doc] = id_send[me_doc]

    loads[3].wait()
    loads[4].wait()
    teach = teach_ref[...]
    t_top = jnp.max(teach, axis=0, keepdims=True)
    t_exp = jnp.exp(teach - t_top)
    t_sum = jnp.sum(t_exp, axis=0, keepdims=True)
    t_weight = t_exp / t_sum
    t_total = t_top + jnp.log(t_sum)
    group = me_doc * nqry + me_qry
    col = jnp.sum(
        jnp.where(lax.broadcasted_iota(I32, pat_ref.shape, 1) == group, pat_ref[...], 0).astype(F32),
        axis=1, keepdims=True,
    )
    nq = teach.shape[1]
    per = nq // nqry
    spread = lax.broadcasted_iota(I32, (nqry, nq), 1) // per == lax.broadcasted_iota(I32, (nqry, nq), 0)
    active = jnp.sum(jnp.where(spread, col, 0.0), axis=0, keepdims=True) > 0.5

    collect(2, 5)
    from_partner(1, 4, 2, 5)
    exchange(q2, send2, recv2, ss_sem.at[1], sr_sem.at[1])

    pltpu.make_async_copy(id_recv.at[pl.ds(0, ndoc - 1)], id_recv.at[pl.ds(0, ndoc - 1)], idr_sem).wait()
    pltpu.make_async_copy(id_send.at[pl.ds(0, ndoc - 1)], id_send.at[pl.ds(0, ndoc - 1)], ids_sem).wait()
    got = id_recv[...].reshape(ndoc, 128).astype(BF16)
    wide = (
        lax.broadcasted_iota(I32, (slots, ndoc), 0) // CAP == lax.broadcasted_iota(I32, (slots, ndoc), 1)
    ).astype(F32).astype(BF16)
    lines = jnp.dot(wide, got, preferred_element_type=F32)
    r_i = lax.broadcasted_iota(I32, (slots, 128), 0)
    l_i = lax.broadcasted_iota(I32, (slots, 128), 1)
    mine = jnp.sum(jnp.where(lax.rem(r_i, CAP) == l_i, lines, 0.0), axis=1, keepdims=True)
    doc = jnp.broadcast_to(mine, (slots, 128)).astype(I32) - 1
    doc_of[...] = doc.reshape(slots // 8, 8, 128)
    hot = (doc == l_i).astype(F32)
    onehot[...] = hot.astype(BF16)
    onehot_t[...] = hot.T.astype(BF16)

    def all_blocks(ref, sem):
        return pltpu.make_async_copy(ref.at[pl.ds(0, ndoc - 1)], ref.at[pl.ds(0, ndoc - 1)], sem)

    def pool(recv):
        def tops(v, best):
            got = jnp.concatenate(
                [recv[2 * v].astype(I32).astype(F32), recv[2 * v + 1].astype(I32).astype(F32)], axis=0
            )
            size = 0.5 * (jnp.exp(jnp.abs(got) / steps) - 1.0)
            val, d = jnp.where(got < 0.0, -size, size), doc_of[v]
            value[v] = val
            return tuple(jnp.maximum(b, jnp.where(d == t, val, LOW)) for t, b in enumerate(best))

        best = lax.fori_loop(
            0, slots // 8, tops, tuple(jnp.full((8, 128), LOW, F32) for _ in range(MAXP)), unroll=8
        )
        for t in range(MAXP):
            top[t : t + 1] = jnp.max(best[t], axis=0, keepdims=True)
        top_b = top[...].astype(BF16)
        pad = jnp.zeros((128 - MAXP, 128), BF16)
        of_row = jnp.dot(onehot[...], jnp.concatenate([top_b, pad], axis=0), preferred_element_type=F32)
        e = jnp.exp(value[...].reshape(slots, 128) - of_row)
        e_hi = e.astype(BF16)
        e_lo = (e - e_hi.astype(F32)).astype(BF16)
        total = jnp.dot(onehot_t[...], e_hi, preferred_element_type=F32) + jnp.dot(
            onehot_t[...], e_lo, preferred_element_type=F32
        )
        return top_b.astype(F32) + jnp.log(total[:MAXP])

    all_blocks(recv1, sr_sem.at[0]).wait()
    pool1 = pool(recv1)
    all_blocks(recv2, sr_sem.at[1]).wait()
    pool2 = pool(recv2)
    lane_p = lax.broadcasted_iota(I32, pool1.shape, 1)
    back_half = lax.rem(lane_p, 2 * half) >= half
    near = jnp.where((lane_p < side) | back_half, pool1, pool2)
    away = jnp.where((lane_p < side) | back_half, pool2, pool1)
    pooled = pltpu.roll(jnp.concatenate([near, away], axis=1), x * side, 1)
    docs_ref[...] = jnp.where(active, pooled, 0.0)

    s_top = jnp.max(pooled, axis=0, keepdims=True)
    s_total = s_top + jnp.log(jnp.sum(jnp.exp(pooled - s_top), axis=0, keepdims=True))
    mean = jnp.sum(t_weight * (teach - pooled), axis=0, keepdims=True)
    s_total = jnp.where(active, s_total, LOW)
    t_tot = jnp.where(active, t_total, LOW)
    mean = jnp.where(active, mean, 0.0)
    fill = jnp.zeros((5, nq), F32)
    stats = jnp.concatenate([s_total, t_tot, mean, fill], axis=0)
    stat[0] = stats[:, :128]
    stat[1] = stats[:, 128:]

    def send_stat(peer, px, pc):
        pltpu.make_async_remote_copy(
            src_ref=stat.at[lax.div(peer * per, 128)], dst_ref=stat_got.at[me_qry], send_sem=xs_sem,
            recv_sem=xr_sem, device_id={"x": px, "c": pc}, device_id_type=MESH,
        ).start()

    each_qry_peer(send_stat)
    stat_got[me_qry] = stat[lax.div(me_qry * per, 128)]
    pltpu.make_async_copy(stat_got.at[pl.ds(0, nqry - 1)], stat_got.at[pl.ds(0, nqry - 1)], xr_sem).wait()
    part = stat_got[...]
    peak = jnp.max(part, axis=0)
    mass = jnp.exp(part - peak[None])
    summed = jnp.sum(mass, axis=0)
    totals = peak + jnp.log(summed)
    mean8 = jnp.sum(mass[:, 1:2] * part[:, 2:3], axis=0) / summed[1:2]
    shift = lax.rem(me_qry * per, 128)
    turn = mod(-shift, 128)
    lane1 = lax.broadcasted_iota(I32, (1, 128), 1)
    r0 = pltpu.roll(totals[0:1], turn, 1)
    r1 = pltpu.roll(totals[1:2], lax.rem(turn + per, 128), 1)
    r2 = pltpu.roll(mean8, lax.rem(turn + 2 * per, 128), 1)
    line = jnp.where(lane1 < per, r0, jnp.where(lane1 < 2 * per, r1, r2))
    row[...] = line
    row_got[me_doc] = line

    def send_row(py, pz):
        pltpu.make_async_remote_copy(
            src_ref=row, dst_ref=row_got.at[me_doc], send_sem=ds_sem, recv_sem=dr_sem,
            device_id={"y": py, "z": pz}, device_id_type=MESH,
        ).start()

    each_doc_peer(send_row)
    pltpu.make_async_copy(row_got.at[pl.ds(0, ndoc - 1)], row_got.at[pl.ds(0, ndoc - 1)], dr_sem).wait()
    rows = row_got[...].reshape(ndoc, 128)
    peak = jnp.max(rows, axis=0, keepdims=True)
    mass = jnp.exp(rows - peak)
    summed = jnp.sum(mass, axis=0, keepdims=True)
    totals = peak + jnp.log(summed)
    weighted = jnp.sum(pltpu.roll(mass, per, 1) * rows, axis=0, keepdims=True)
    at2 = weighted / pltpu.roll(summed, per, 1)
    out = pltpu.roll(at2, 128 - 2 * per, 1) - pltpu.roll(totals, 128 - per, 1) + totals
    div_ref[...] = out[:, :per]

    all_blocks(recv1, ss_sem.at[0]).wait()
    all_blocks(recv2, ss_sem.at[1]).wait()
    for t in sends:
        t.wait_send()
    pltpu.make_async_copy(stat_got.at[pl.ds(0, nqry - 1)], stat_got.at[pl.ds(0, nqry - 1)], xs_sem).wait()
    pltpu.make_async_copy(row_got.at[pl.ds(0, ndoc - 1)], row_got.at[pl.ds(0, ndoc - 1)], ds_sem).wait()


def hand_on(docs_ref, div_ref, docs_out, div_out, sem):
    copies = [
        pltpu.make_async_copy(docs_ref, docs_out, sem.at[0]),
        pltpu.make_async_copy(div_ref, div_out, sem.at[1]),
    ]
    for copy in copies:
        copy.start()
    for copy in copies:
        copy.wait()


def on_device(ny, nz, nx, queries, passages, route, pattern, teacher):
    ndoc, nqry = ny * nz, nx * 2
    npass, dim = passages.shape
    rows_dev = queries.shape[0]
    nq, docs = teacher.shape
    vmem = pl.BlockSpec(memory_space=pltpu.VMEM)
    hbm = pl.BlockSpec(memory_space=pltpu.HBM)
    dma, regular = pltpu.SemaphoreType.DMA, pltpu.SemaphoreType.REGULAR
    inputs = (queries, passages, route.reshape(1, npass), pattern, teacher.T)
    pooled, divergence = pl.pallas_call(
        functools.partial(kernel, ny, nz, nx),
        out_shape=(
            jax.ShapeDtypeStruct((docs, nq), F32),
            jax.ShapeDtypeStruct((1, rows_dev), F32),
        ),
        in_specs=[hbm] * 5,
        out_specs=(vmem, vmem),
        scratch_shapes=[
            pltpu.VMEM((npass, dim), BF16),
            pltpu.VMEM((1, npass), I32),
            pltpu.VMEM(pattern.shape, I32),
            pltpu.VMEM((docs, nq), F32),
            pltpu.VMEM((nq // 2, dim), BF16),
            pltpu.VMEM((nq // 2, dim), BF16),
            pltpu.VMEM((ndoc * CAP, dim), BF16),
            pltpu.VMEM((ndoc, CAP, 128), jnp.int16),
            pltpu.VMEM((ndoc, CAP, 128), jnp.int16),
            pltpu.VMEM((ndoc, CAP, 128), jnp.int16),
            pltpu.VMEM((ndoc, CAP, 128), jnp.int16),
            pltpu.VMEM((ndoc * CAP // 8, 8, 128), F32),
            pltpu.VMEM((ndoc, 1, 128), F32),
            pltpu.VMEM((ndoc, 1, 128), F32),
            pltpu.VMEM((ndoc * CAP // 8, 8, 128), I32),
            pltpu.VMEM((ndoc * CAP, 128), BF16),
            pltpu.VMEM((128, ndoc * CAP), BF16),
            pltpu.VMEM((MAXP, 128), F32),
            pltpu.VMEM((2, 8, 128), F32),
            pltpu.VMEM((nqry, 8, 128), F32),
            pltpu.VMEM((1, 128), F32),
            pltpu.VMEM((ndoc, 1, 128), F32),
            dma((5,)), regular, regular, regular,
            dma((6,)), dma((6,)), dma((7,)), dma((7,)),
            dma, dma, dma((2,)), dma((2,)), dma, dma, dma, dma,
        ],
        compiler_params=pltpu.CompilerParams(
            collective_id=0, has_side_effects=True, vmem_limit_bytes=32 * 1024 * 1024
        ),
    )(*(pltpu.with_memory_space_constraint(a, pltpu.HBM) for a in inputs))
    pooled, divergence = pl.pallas_call(
        hand_on,
        out_shape=(
            jax.ShapeDtypeStruct((docs, nq), F32),
            jax.ShapeDtypeStruct((1, rows_dev), F32),
        ),
        in_specs=[pl.BlockSpec(memory_space=pl.ANY)] * 2,
        out_specs=(hbm, hbm),
        scratch_shapes=[dma((2,))],
        compiler_params=pltpu.CompilerParams(vmem_limit_bytes=1024 * 1024),
    )(pooled, divergence)
    return pooled.T, divergence.reshape(rows_dev)


def solution(mesh):
    split = Mesh(mesh.devices.reshape(4, -1, 4, 2), AXES)
    ny, nz, nx = (split.shape[a] for a in ("y", "z", "x"))
    placed = (P(("x", "c"), None), P(AXES, None), P(AXES), P(), P(None, AXES))
    return jax.shard_map(
        functools.partial(on_device, ny, nz, nx),
        mesh=split,
        in_specs=placed,
        out_specs=(P(None, AXES), P(("x", "c"))),
        check_vma=False,
    )
```
